32 devices in a mesh: dp: 2 (over y), ctx: 4 (over z), exp: 4 (over x, core).
Axes of the slice: x: 2, y: 2, z: 4, core: 2. Of those that a mesh axis runs over, the one named last changes fastest.
Arguments:
- queries: bfloat16 [8, 512, 2048], P(('dp', 'exp'), 'ctx'), may hold values from -24 to 24
- keys: bfloat16 [8, 512, 2048], P(('dp', 'exp'), 'ctx'), may hold values from -20 to 20
- values: bfloat16 [8, 512, 2048], P(('dp', 'exp'), 'ctx'), may hold values from -6 to 6
- resid: bfloat16 [8, 512, 2048], P(('dp', 'exp'), 'ctx'), may hold values from -3 to 3
- norm_gain: float32 [2048], replicated, may hold values from 0.5 to 1.5
- expert_ids: int32 [8, 512, 8], P(('dp', 'exp'), 'ctx'), may hold values from 0 to 15, all different within a row; in each aligned block of 128 rows (0 to 127, 128 to 255, ..., all dimensions but the last counted through in order) at most 68 rows name the same one
- gate_weights: float32 [8, 512, 8], P(('dp', 'exp'), 'ctx'), may hold values from 0.05 to 0.5
- mask_flags: int32 [8, 512], P(('dp', 'exp'), 'ctx'), may hold values 0 or 1
- cotangent: bfloat16 [8, 512, 2048], P(('dp', 'exp'), 'ctx'), may hold values from -0.59765625 to 0.59765625
- w_gate_up: bfloat16 [16, 2048, 1024], P(('ctx', 'exp')), may hold values from -0.125 to 0.125
- w_down: bfloat16 [16, 2048, 512], P(('ctx', 'exp')), may hold values from -0.25 to 0.25
Outputs:
- stream: bfloat16 [8, 512, 2048], P(('dp', 'exp'), 'ctx')
- grad_gate_up: float32 [16, 2048, 1024], P(('ctx', 'exp'), 'dp')
- grad_down: float32 [16, 2048, 512], P(('ctx', 'exp'), 'dp')
The draws below stay inside these ranges and needn't reach their ends.
Inputs may be any that keep to these rules, and one draw needn't show every extreme that they name: `expert_ids`: in the rows of one device no expert is named more than 68 times, and some device names some expert exactly 68 times.
All inputs are finite; a program needn't handle non-finite values. No bound on the sum of `mask_flags` on one device may be relied on, other than what follows from the above.
Results may differ from the reference program's by a relative error of at most 0.0088.
Values may be sent and summed in bfloat16 or wider, within the bound.
No kernel may reach another device: no remote copies, remote signals or barrier semaphores. Data moves between devices by JAX's collectives and lax.ppermute only.
A program may use at most 128 MiB of HBM per device.

```python
import math
import jax
import jax.numpy as jnp
import numpy as np
from jax import lax

D = 2048
HEADS = 16
HEAD_DIM = 128
FW = 512
TOP = 8
TOK_DEV = 128
EXPERTS = 16
CAP = 68
LEN = 512
BATCH = 8
N_DP = 2
N_CTX = 4
N_EXP = 4


def key_base(key):
    noise = jax.random.normal(jax.random.fold_in(key, 11), (BATCH, LEN, D), jnp.float32)
    return 1.6 * jnp.clip(noise, -5.0, 5.0)


def draw_keys(key, part):
    base = key_base(key)
    return base.astype(jnp.bfloat16)


def draw_queries(key, part):
    noise = jax.random.normal(jax.random.fold_in(key, 23), (BATCH, LEN, D), jnp.float32)
    own = 1.6 * jnp.clip(noise, -5.0, 5.0)
    return own.astype(jnp.bfloat16)


def with_ends(result, stream_key, low, high):
    longest = result.shape.index(max(result.shape))
    spots = []
    for shift in (0, 1):
        where = [jax.random.randint(jax.random.fold_in(stream_key, axis), (), 0, length) for axis, length in enumerate(result.shape)]
        where[longest] = (where[longest] + shift) % result.shape[longest]
        spots.append(tuple(where))
    return result.at[spots[0]].set(low).at[spots[1]].set(high)


def levels(rng, dims, split, low, high):
    def one(dim, shards_of):
        heights = jax.random.uniform(jax.random.fold_in(jax.random.fold_in(rng, 6), dim), (shards_of,), jnp.float32, low / len(split), high / len(split))
        return jnp.repeat(jnp.exp(heights), dims[dim] // shards_of).reshape((-1,) + (1,) * (len(dims) - dim - 1))

    loudness = one(*split[0])
    for cut in split[1:]:
        loudness = loudness * one(*cut)
    return loudness


def routed_block(key, own, number, rows, count, top, most, skew):
    order = jax.random.permutation(key, count)
    packed, common = shares(count, rows * top, most, skew, True), shares(count, rows * top, most, skew, False)
    places = jnp.arange(count)

    def named(lengths, rotation):
        used = int((lengths > 0).sum())
        fixed = max(1, used // 4)
        passed = fixed + (places - fixed + rotation * (used - fixed)) % max(1, count - fixed)
        return jnp.zeros((count,), jnp.int32).at[order[jnp.where(places < fixed, places, passed)]].set(jnp.asarray(lengths, jnp.int32))

    lengths = jnp.where(number % 4 == 0, named(packed, number // 4), named(common, number - number // 4 - 1))
    mixed = jax.random.permutation(jax.random.fold_in(own, 3), count)
    source_of, receiver = mixed[0:count // 2 * 2:2], mixed[1:count // 2 * 2:2]
    room = jnp.minimum(lengths[source_of] - 1, most - lengths[receiver]) // 2
    room = jnp.where((source_of == order[0]) | (receiver == order[0]) | (lengths[receiver] == 0), 0, jnp.maximum(room, 0))
    passed = jax.random.randint(jax.random.fold_in(own, 4), (count // 2,), 0, 1 << 20) % (room + 1)
    lengths = lengths.at[source_of].add(-passed).at[receiver].add(passed)
    items = jnp.searchsorted(jnp.cumsum(lengths), jnp.arange(rows * top), side="right").astype(jnp.int32)
    table = items.reshape(top, rows).T
    table = table[jax.random.permutation(jax.random.fold_in(own, 1), rows)]
    rotation = jax.random.randint(jax.random.fold_in(own, 2), (rows, 1), 0, top)
    return jnp.take_along_axis(table, (jnp.arange(top)[None, :] + rotation) % top, axis=1)


def shares(amount, total, reach, skew, full):
    portions = [(1 << 20) // math.isqrt(standing ** skew) + 1 for standing in range(1, amount + 1)]
    largest = reach if full else min(reach, max(-(-total // amount), total * portions[0] // sum(portions)))
    least = 1 if total - largest >= amount - 1 else 0
    holding, spare = [largest] + [least] * (amount - 1), total - largest - least * (amount - 1)
    while spare > 0:
        free = [i for i in range(1, amount) if holding[i] < largest] or [i for i in range(1, amount) if holding[i] < reach]
        mass, remaining = sum([portions[i] for i in free]), spare
        for i in free:
            more = min(reach - holding[i], max(1, remaining * portions[i] // mass), spare)
            holding[i] = holding[i] + more
            spare = spare - more
    return np.array(holding)


def normal_values(stream_key, dims, deviation, limit, shards=(), kind=jnp.bfloat16):
    factor_of = levels(stream_key, dims, shards, -0.22, 0.18) if shards else 1.0
    values = jax.random.normal(stream_key, dims, jnp.float32) * deviation * factor_of
    return jnp.minimum(jnp.maximum(values, -limit), limit).astype(kind)


def setup_inputs(seed: int = 0) -> dict:
    seeds = jax.random.split(jax.random.key(seed), 12)
    queries = draw_queries(jax.random.fold_in(seeds[11], 71), 0)
    keys = draw_keys(jax.random.fold_in(seeds[11], 71), 0)
    values = normal_values(seeds[2], (BATCH, LEN, D), 1.0, 6.0, ((0, 8), (1, 4)))
    resid = normal_values(seeds[3], (BATCH, LEN, D), 0.5, 3.0, ((0, 8), (1, 4)))
    norm_gain = jnp.clip(1.0 + 0.1 * jax.random.normal(seeds[4], (D,), jnp.float32), 0.5, 1.5)
    expert_ids_keys = jax.random.split(jax.random.fold_in(seeds[5], 1), BATCH * LEN // TOK_DEV)
    expert_ids_turns = jax.random.permutation(jax.random.fold_in(seeds[5], 3), BATCH * LEN // TOK_DEV)
    expert_ids = jax.vmap(lambda own, number: routed_block(jax.random.fold_in(seeds[5], 2), own, number, TOK_DEV, EXPERTS, TOP, CAP, 2))(expert_ids_keys, expert_ids_turns).reshape((BATCH, LEN, TOP))
    gate_weights = jnp.clip(jnp.exp(math.log(0.5) - 2.3025851 * jax.random.uniform(seeds[6], (BATCH, LEN, TOP), jnp.float32) ** levels(seeds[6], (BATCH, LEN, TOP), ((0, 8), (1, 4)), -0.2, 0.2)), 0.05, 0.5)
    mask_flags = with_ends((jax.random.randint(seeds[7], (BATCH, LEN), 0, 2) < 1).astype(jnp.int32), jax.random.fold_in(seeds[7], 1), 0, 1)
    cotangent = normal_values(seeds[8], (BATCH, LEN, D), 0.1, 0.59765625, ((0, 8), (1, 4)))
    w_gate_up = normal_values(seeds[9], (EXPERTS, D, 2 * FW), D ** -0.5, 0.125, ((0, 16),))
    w_down = normal_values(seeds[10], (EXPERTS, D, FW), FW ** -0.5, 0.25, ((0, 16),))
    return dict(queries=queries, keys=keys, values=values, resid=resid, norm_gain=norm_gain, expert_ids=expert_ids, gate_weights=gate_weights, mask_flags=mask_flags, cotangent=cotangent, w_gate_up=w_gate_up, w_down=w_down)


def attend_ref(query_seq, key_seq, value_seq):
    length = query_seq.shape[0]
    query_heads = query_seq.astype(jnp.float32).reshape(length, HEADS, HEAD_DIM)
    key_heads = key_seq.astype(jnp.float32).reshape(length, HEADS, HEAD_DIM)
    value_heads = value_seq.astype(jnp.float32).reshape(length, HEADS, HEAD_DIM)
    scores = jnp.einsum('qhd,khd->hqk', query_heads, key_heads) / jnp.sqrt(jnp.float32(HEAD_DIM))
    largest = lax.optimization_barrier(jnp.max(scores, axis=2, keepdims=True))
    powers = jnp.exp(scores - largest)
    probs = (powers / lax.optimization_barrier(jnp.sum(powers, axis=2, keepdims=True))).astype(jnp.bfloat16)
    attended = jnp.einsum('hqk,khd->qhd', probs.astype(jnp.float32), value_heads)
    return attended.reshape(length, HEADS * HEAD_DIM)

def rms_normed(stream, norm_gain):
    widened = lax.optimization_barrier(stream).astype(jnp.float32)
    factor = lax.rsqrt(lax.optimization_barrier(jnp.mean(widened * widened, axis=-1, keepdims=True)) + 1e-05)
    return (widened * factor * norm_gain.astype(jnp.float32)).astype(jnp.bfloat16)

def slot_targets(routes, experts, capacity):
    flat_ids = routes.reshape(-1).astype(jnp.int32)
    onehot = (flat_ids[:, None] == jnp.arange(experts, dtype=jnp.int32)[None, :]).astype(jnp.int32)
    ranks = jnp.cumsum(onehot, axis=0).astype(jnp.int32) - 1
    within = lax.optimization_barrier(jnp.sum(ranks * onehot, axis=1)).astype(jnp.int32)
    return flat_ids * capacity + within

def pack_rows(normed, cot_rows, routes, gates, flags, experts, capacity):
    tokens = normed.shape[0]
    model_width = normed.shape[1]
    top_count = routes.shape[1]
    targets = slot_targets(routes, experts, capacity)
    scaled = cot_rows.astype(jnp.float32)[:, None, :] * gates.astype(jnp.float32)[:, :, None] * flags.astype(jnp.float32)[:, None, None]
    grad_rows = scaled.astype(jnp.bfloat16).reshape(tokens * top_count, model_width)
    input_rows = jnp.repeat(normed, top_count, axis=0)
    empty = jnp.zeros((experts * capacity, model_width), jnp.bfloat16)
    return (empty.at[targets].set(input_rows), empty.at[targets].set(grad_rows))

def expert_term(input_rows, grad_rows, gate_up, down_map):
    hidden_width = down_map.shape[1]
    projected = jnp.dot(input_rows, gate_up, preferred_element_type=jnp.float32)
    gate_part = projected[:, :hidden_width]
    up_part = projected[:, hidden_width:]
    sigma = jax.nn.sigmoid(gate_part)
    activated = gate_part * sigma
    hidden = (activated * up_part).astype(jnp.bfloat16)
    back_hidden = jnp.dot(grad_rows, down_map, preferred_element_type=jnp.float32)
    slope = sigma * (1.0 + gate_part * (1.0 - sigma))
    back_both = jnp.concatenate([back_hidden * up_part * slope, back_hidden * activated], axis=1).astype(jnp.bfloat16)
    return (hidden, back_both)

def term_rows(input_rows, grad_rows, hidden, back_both, first_row, row_count):
    inputs_cut = lax.dynamic_slice_in_dim(input_rows, first_row, row_count, 1)
    grads_cut = lax.dynamic_slice_in_dim(grad_rows, first_row, row_count, 1)
    contract = (((0,), (0,)), ((), ()))
    left_part = lax.dot_general(inputs_cut, back_both, contract, preferred_element_type=jnp.float32)
    right_part = lax.dot_general(grads_cut, hidden, contract, preferred_element_type=jnp.float32)
    return jnp.concatenate([left_part, right_part], axis=1)

def reference(queries, keys, values, resid, norm_gain, expert_ids, gate_weights, mask_flags, cotangent, w_gate_up, w_down):

    def one_sequence(items):
        query_seq, key_seq, value_seq, resid_seq = items
        attended = attend_ref(query_seq, key_seq, value_seq)
        return (resid_seq.astype(jnp.float32) + attended).astype(jnp.bfloat16)
    stream = lax.map(one_sequence, (queries, keys, values, resid))
    normed = rms_normed(stream, norm_gain)
    sources = N_CTX * N_EXP
    total = jnp.zeros((EXPERTS, D, 3 * FW), jnp.float32)
    for group in range(N_DP):
        lower = group * N_EXP
        upper = lower + N_EXP

        def blocks(array):
            piece = array[lower:upper]
            rest = piece.shape[2:]
            piece = piece.reshape((N_EXP, N_CTX, TOK_DEV) + rest)
            piece = jnp.swapaxes(piece, 0, 1)
            return piece.reshape((sources, TOK_DEV) + rest)

        def pack_block(normed_blk, cot_blk, ids_blk, gates_blk, flags_blk):
            return pack_rows(normed_blk, cot_blk, ids_blk, gates_blk, flags_blk, EXPERTS, CAP)
        input_all, grad_all = jax.vmap(pack_block)(blocks(normed), blocks(cotangent), blocks(expert_ids), blocks(gate_weights), blocks(mask_flags))

        def by_expert(array):
            array = array.reshape(sources, EXPERTS, CAP, D)
            return jnp.swapaxes(array, 0, 1).reshape(EXPERTS, sources * CAP, D)

        def one_expert(items):
            input_rows, grad_rows, gate_up, down_map = items
            hidden, back_both = expert_term(input_rows, grad_rows, gate_up, down_map)
            return term_rows(input_rows, grad_rows, hidden, back_both, 0, D)
        partial_sum = lax.map(one_expert, (by_expert(input_all), by_expert(grad_all), w_gate_up, w_down))
        rounded = lax.optimization_barrier(partial_sum.astype(jnp.bfloat16)).astype(jnp.float32)
        total = total + rounded
    return (stream, total[:, :, :2 * FW], total[:, :, 2 * FW:])
```

```python
import math

import jax
import jax.numpy as jnp
from jax import lax
from jax.experimental import pallas as pl
from jax.experimental.pallas import tpu as pltpu
from jax.sharding import PartitionSpec as P

HEAD_DIM = 128
F32 = jnp.float32
BF16 = jnp.bfloat16
VMEM_LIMIT = 56 * 1024 * 1024


def attend_kernel(place, *refs, ctx, tokens, width):
    packs, out = refs[:ctx], refs[ctx]
    z = place[0]
    scale = 1.0 / math.sqrt(HEAD_DIM)
    nt = (((1,), (1,)), ((), ()))
    nn = (((1,), (0,)), ((), ()))
    for h in range(width // HEAD_DIM):
        cols = slice(h * HEAD_DIM, (h + 1) * HEAD_DIM)
        q, k, v = (
            jnp.concatenate([p[i, :, cols] for p in packs], axis=0) for i in range(3)
        )
        scores = lax.dot_general(q, k, nt, preferred_element_type=F32) * scale
        largest = jnp.max(scores, axis=1, keepdims=True)
        powers = jnp.exp(scores - largest)
        probs = (powers / jnp.sum(powers, axis=1, keepdims=True)).astype(BF16)
        attended = lax.dot_general(probs, v, nn, preferred_element_type=F32)
        for s in range(ctx):
            first = pl.multiple_of(lax.rem(z - s + ctx, ctx) * tokens, tokens)
            rows = packs[s][3, :, cols].astype(F32) + attended[s * tokens : (s + 1) * tokens]
            out[pl.ds(first, tokens), cols] = rows.astype(BF16)


def attend(place, packs):
    ctx = len(packs)
    _, tokens, width = packs[0].shape
    vmem = pl.BlockSpec(memory_space=pltpu.VMEM)
    return pl.pallas_call(
        lambda *refs: attend_kernel(*refs, ctx=ctx, tokens=tokens, width=width),
        out_shape=jax.ShapeDtypeStruct((ctx * tokens, width), BF16),
        in_specs=[pl.BlockSpec(memory_space=pltpu.SMEM)] + [vmem] * ctx,
        out_specs=vmem,
        compiler_params=pltpu.CompilerParams(vmem_limit_bytes=VMEM_LIMIT),
        name="attend",
    )(place, *packs)


def expert_kernel(place, gates, gain, gate_up, down, *refs, seqs, ctx, exp, cap, parts, with_stream):
    slices = [refs[i * ctx : (i + 1) * ctx] for i in range(seqs)]
    cots = [refs[(seqs + i) * ctx : (seqs + i + 1) * ctx] for i in range(seqs)]
    rest = refs[2 * seqs * ctx :]
    norm_out, cot_out, back_out, hidden_out = rest[:4]
    stream_out = rest[4] if with_stream else None
    rows_ref, cot_ref, gate_ref, mine_ref = rest[-4:]
    tokens, width_all = cots[0][0].shape
    width = width_all // ctx
    half = width_all // parts
    hidden_width = down.shape[1]
    z, part = place[0], place[1]
    nn = (((1,), (0,)), ((), ()))
    lower = lax.broadcasted_iota(jnp.int32, (tokens, tokens), 0)
    upper = lax.broadcasted_iota(jnp.int32, (tokens, tokens), 1)
    running = (lower <= upper).astype(BF16)
    row_number = lax.broadcasted_iota(jnp.int32, (cap, tokens), 0).astype(F32)
    sources = [lax.rem(z - s + ctx, ctx) for s in range(ctx)]
    if with_stream:
        for s in range(ctx):
            first = pl.multiple_of(z * tokens, tokens)
            mine_ref[sources[s]] = slices[0][s][pl.ds(first, tokens), :]
        for s in range(ctx):
            stream_out[:, s * width : (s + 1) * width] = mine_ref[s]
    for i in range(seqs):
        for s in range(ctx):
            first = pl.multiple_of(sources[s] * tokens, tokens)
            gate = gates[sources[s] * exp + place[2 + i]]
            picked = gate != 0.0
            marks = jnp.broadcast_to(picked.astype(F32), (8, tokens)).astype(BF16)
            rank = lax.dot_general(marks, running, nn, preferred_element_type=F32)[:1]
            chosen = jnp.logical_and(row_number + 1.0 == rank, picked)
            select = chosen.astype(F32).astype(BF16)
            at = (i * ctx + s) * cap
            gate_ref[at : at + cap, :] = jnp.broadcast_to(
                jnp.sum(jnp.where(chosen, gate, 0.0), axis=1, keepdims=True), (cap, 128)
            )
            for f in range(ctx):
                block = slices[i][f][pl.ds(first, tokens), :]
                rows = lax.dot_general(select, block, nn, preferred_element_type=F32)
                rows_ref[sources[f], at : at + cap, :] = rows.astype(BF16)
            for p in range(parts):
                block = cots[i][s][:, p * half : (p + 1) * half]
                rows = lax.dot_general(select, block, nn, preferred_element_type=F32)
                cot_ref[p, at : at + cap, :] = rows.astype(BF16)
    total = None
    for f in range(ctx):
        wide = rows_ref[f].astype(F32)
        square = jnp.sum(wide * wide, axis=1, keepdims=True)
        total = square if total is None else total + square
    factor = lax.rsqrt(total / width_all + 1e-05)
    proj = None
    for f in range(ctx):
        normed = (rows_ref[f].astype(F32) * factor * gain[f]).astype(BF16)
        rows_ref[f] = normed
        term = lax.dot_general(
            normed, gate_up[f * width : (f + 1) * width, :], nn, preferred_element_type=F32
        )
        proj = term if proj is None else proj + term
    back = None
    for p in range(parts):
        term = lax.dot_general(
            cot_ref[p], down[p * half : (p + 1) * half, :], nn, preferred_element_type=F32
        )
        back = term if back is None else back + term
    gate_column = gate_ref[:, :1]
    gate_part, up_part = proj[:, :hidden_width], proj[:, hidden_width:]
    sigma = 1.0 / (1.0 + jnp.exp(-gate_part))
    activated = gate_part * sigma
    back = back * gate_column
    hidden_out[...] = (activated * up_part * gate_column).astype(BF16)
    slope = sigma * (1.0 + gate_part * (1.0 - sigma))
    back_out[:, :hidden_width] = (back * up_part * slope).astype(BF16)
    back_out[:, hidden_width:] = (back * activated).astype(BF16)
    cot_out[...] = cot_ref[part]
    each = ctx // parts
    for f in range(each):
        norm_out[:, f * width : (f + 1) * width] = rows_ref[part * each + f]


def expert_rows(place, gates, gain, gate_up, down, slices, cots, cap, exp, parts, with_stream):
    seqs, ctx = len(slices), len(slices[0])
    tokens, width_all = cots[0][0].shape
    width = width_all // ctx
    half = width_all // parts
    hidden_width = down.shape[1]
    count = seqs * ctx * cap
    vmem = pl.BlockSpec(memory_space=pltpu.VMEM)
    shapes = [
        jax.ShapeDtypeStruct((count, half), BF16),
        jax.ShapeDtypeStruct((count, half), BF16),
        jax.ShapeDtypeStruct((count, 2 * hidden_width), BF16),
        jax.ShapeDtypeStruct((count, hidden_width), BF16),
    ]
    if with_stream:
        shapes.append(jax.ShapeDtypeStruct((tokens, width_all), BF16))
    args = [a for one in slices for a in one] + [a for one in cots for a in one]
    return pl.pallas_call(
        lambda *refs: expert_kernel(
            *refs, seqs=seqs, ctx=ctx, exp=exp, cap=cap, parts=parts, with_stream=with_stream
        ),
        out_shape=shapes,
        in_specs=[pl.BlockSpec(memory_space=pltpu.SMEM)] + [vmem] * (4 + len(args)),
        out_specs=[vmem] * len(shapes),
        scratch_shapes=[
            pltpu.VMEM((ctx, count, width), BF16),
            pltpu.VMEM((parts, count, half), BF16),
            pltpu.VMEM((count, 128), F32),
            pltpu.VMEM((ctx, tokens, width), BF16),
        ],
        compiler_params=pltpu.CompilerParams(vmem_limit_bytes=VMEM_LIMIT),
        name="expert_rows",
    )(place, gates, gain, gate_up, down, *args)


def grads_kernel(*refs, groups, add):
    norms, cots, backs, hiddens = (refs[i * groups : (i + 1) * groups] for i in range(4))
    rest = refs[4 * groups :]
    tn = (((0,), (0,)), ((), ()))

    def whole(parts):
        return jnp.concatenate([p[...] for p in parts], axis=0)

    left = lax.dot_general(whole(norms), whole(backs), tn, preferred_element_type=F32)
    right = lax.dot_general(whole(cots), whole(hiddens), tn, preferred_element_type=F32)
    out_left, out_right = rest[-2:]
    if add:
        left = left + rest[0][0]
        right = right + rest[1][0]
    out_left[0] = left
    out_right[0] = right


def grads(pieces, before):
    groups = len(pieces)
    norms, cots, backs, hiddens = zip(*pieces)
    count, half = norms[0].shape
    step = 256
    tall = [pl.BlockSpec((count, step), lambda i: (0, i))] * groups
    out_widths = (backs[0].shape[1], hiddens[0].shape[1])
    full = [
        pl.BlockSpec((count, w), lambda i: (0, 0)) for w in out_widths for _ in range(groups)
    ]
    outs = [pl.BlockSpec((1, step, w), lambda i: (0, i, 0)) for w in out_widths]
    add = before is not None
    args = [*norms, *cots, *backs, *hiddens] + (list(before) if add else [])
    return pl.pallas_call(
        lambda *refs: grads_kernel(*refs, groups=groups, add=add),
        out_shape=[jax.ShapeDtypeStruct((1, half, w), F32) for w in out_widths],
        grid=(half // step,),
        in_specs=tall + tall + full + (outs if add else []),
        out_specs=outs,
        input_output_aliases={4 * groups: 0, 4 * groups + 1: 1} if add else {},
        compiler_params=pltpu.CompilerParams(vmem_limit_bytes=VMEM_LIMIT),
        name="grads",
    )(*args)


def shifted(value, axis, step, count):
    return lax.ppermute(value, axis, [(i, (i + step) % count) for i in range(count)])


def flipped(value, axis, mask, count):
    return lax.ppermute(value, axis, [(i, i ^ mask) for i in range(count)])


def spread(own, ctx, exp):
    found = {}
    column = [own] + [shifted(own, "ctx", s, ctx) for s in range(1, ctx)]
    found[0, 0] = column
    found[0, 1] = [flipped(b, "exp", 2, exp) for b in column]
    found[1, 0] = [flipped(b, "dp", 1, 2) for b in column]
    found[1, 1] = [
        flipped(found[0, 1][s], "dp", 1, 2) if s % 2 == 0 else flipped(found[1, 0][s], "exp", 2, exp)
        for s in range(ctx)
    ]
    everywhere = {}
    for (dy, dx), blocks in found.items():
        everywhere[dy, dx, 0] = blocks
        everywhere[dy, dx, 1] = [flipped(b, "exp", 1, exp) for b in blocks]
    return everywhere


def expert_gates(routes, gates, flags, experts):
    named = routes[:, :, None] == jnp.arange(experts, dtype=jnp.int32)[None, None, :]
    scaled = gates * flags.astype(F32)[:, None]
    return jnp.sum(jnp.where(named, scaled[:, :, None], 0.0), axis=1)


def per_device(
    queries, keys, values, resid, norm_gain, expert_ids, gate_weights, mask_flags, cotangent, w_gate_up, w_down
):
    ctx, exp, parts = (lax.axis_size(a) for a in ("ctx", "exp", "dp"))
    z, e, part = (lax.axis_index(a) for a in ("ctx", "exp", "dp"))
    experts = ctx * exp
    _, tokens, width_all = queries.shape
    width = width_all // ctx
    most = min(tokens, tokens * expert_ids.shape[2] * 17 // (16 * experts))
    cap = -(-most // 16) * 16

    parts4 = jnp.stack([queries[0], keys[0], values[0], resid[0]])
    parts4 = parts4.reshape(4, tokens, ctx, width).transpose(2, 0, 1, 3)
    packs = []
    for s in range(ctx):
        piece = lax.dynamic_index_in_dim(parts4, lax.rem(z + s, ctx), 0, keepdims=False)
        packs.append(piece if s == 0 else shifted(piece, "ctx", s, ctx))

    by_expert = expert_gates(expert_ids[0], gate_weights[0], mask_flags[0], experts)
    gates_here = lax.all_to_all(
        by_expert.T.reshape(experts, 1, tokens), ("ctx", "exp"), split_axis=0, concat_axis=0, tiled=True
    )
    gates_there = flipped(gates_here, "dp", 1, 2)

    cots = spread(cotangent[0], ctx, exp)
    own_slice = attend(jnp.stack([z, z]), packs)
    streams = spread(own_slice, ctx, exp)

    gain = norm_gain.reshape(ctx, 1, width)
    pieces, stream = [], None
    for dy, dx in ((0, 0), (0, 1), (1, 0), (1, 1)):
        place = jnp.stack([z, part, e ^ (2 * dx), e ^ (2 * dx) ^ 1]).astype(jnp.int32)
        got = expert_rows(
            place,
            gates_there if dy else gates_here,
            gain,
            w_gate_up[0],
            w_down[0],
            [streams[dy, dx, c] for c in range(2)],
            [cots[dy, dx, c] for c in range(2)],
            cap,
            exp,
            parts,
            (dy, dx) == (0, 0),
        )
        if stream is None:
            stream = got[4]
        pieces.append(got[:4])
    first = grads(pieces[:2], None)
    left, right = grads(pieces[2:], first)
    return stream[None], left, right


def routed_device(
    queries, keys, values, resid, norm_gain, expert_ids, gate_weights, mask_flags, cotangent, w_gate_up, w_down
):
    ctx, exp = (lax.axis_size(a) for a in ("ctx", "exp"))
    experts = ctx * exp
    _, tokens, width_all = queries.shape
    top = expert_ids.shape[2]
    capacity = min(tokens, tokens * top * 17 // (16 * experts))
    keys_all = lax.all_gather(keys[0], "ctx", axis=0, tiled=True)
    values_all = lax.all_gather(values[0], "ctx", axis=0, tiled=True)
    heads = width_all // HEAD_DIM
    q, k, v = (a.reshape(-1, heads, HEAD_DIM) for a in (queries[0], keys_all, values_all))
    scores = jnp.einsum("qhd,khd->hqk", q, k, preferred_element_type=F32) / math.sqrt(HEAD_DIM)
    powers = jnp.exp(scores - jnp.max(scores, axis=2, keepdims=True))
    probs = (powers / jnp.sum(powers, axis=2, keepdims=True)).astype(BF16)
    attended = jnp.einsum("hqk,khd->qhd", probs, v, preferred_element_type=F32)
    stream = (resid[0].astype(F32) + attended.reshape(tokens, width_all)).astype(BF16)
    wide = lax.optimization_barrier(stream).astype(F32)
    factor = lax.rsqrt(jnp.mean(wide * wide, axis=-1, keepdims=True) + 1e-05)
    normed = (wide * factor * norm_gain).astype(BF16)

    by_expert = expert_gates(expert_ids[0], gate_weights[0], mask_flags[0], experts)
    picked = by_expert != 0.0
    running = jnp.arange(tokens)[:, None] >= jnp.arange(tokens)[None, :]
    rank = jnp.dot(running.astype(BF16), picked.astype(BF16), preferred_element_type=F32) - 1.0
    slot = jnp.arange(capacity, dtype=F32)[None, :, None]
    chosen = jnp.logical_and(rank.T[:, None, :] == slot, picked.T[:, None, :])
    select = chosen.astype(BF16).reshape(experts * capacity, tokens)
    sent_rows = jnp.dot(select, normed, preferred_element_type=F32).astype(BF16)
    gate_rows = jnp.sum(jnp.where(chosen, by_expert.T[:, None, :], 0.0), axis=2).reshape(-1, 1)
    picked_cot = jnp.dot(select, cotangent[0], preferred_element_type=F32)
    sent_grads = (picked_cot * gate_rows).astype(BF16)

    def exchanged(rows):
        rows = rows.reshape(experts, capacity, width_all)
        got = lax.all_to_all(rows, ("ctx", "exp"), split_axis=0, concat_axis=0, tiled=True)
        return got.reshape(-1, width_all)

    input_rows, grad_rows = exchanged(sent_rows), exchanged(sent_grads)
    hidden_width = w_down.shape[2]
    proj = jnp.dot(input_rows, w_gate_up[0], preferred_element_type=F32)
    gate_part, up_part = proj[:, :hidden_width], proj[:, hidden_width:]
    sigma = jax.nn.sigmoid(gate_part)
    activated = gate_part * sigma
    hidden = (activated * up_part).astype(BF16)
    back = jnp.dot(grad_rows, w_down[0], preferred_element_type=F32)
    slope = sigma * (1.0 + gate_part * (1.0 - sigma))
    both = jnp.concatenate([back * up_part * slope, back * activated], axis=1).astype(BF16)
    tn = (((0,), (0,)), ((), ()))
    left = lax.dot_general(input_rows, both, tn, preferred_element_type=F32)
    right = lax.dot_general(grad_rows, hidden, tn, preferred_element_type=F32)
    partial = jnp.concatenate([left, right], axis=1).astype(BF16)
    summed = lax.psum_scatter(partial, "dp", scatter_dimension=0, tiled=True).astype(F32)
    return stream[None], summed[None, :, : 2 * hidden_width], summed[None, :, 2 * hidden_width :]


def solution(mesh):
    rows = P(("dp", "exp"), "ctx", None)
    weights = P(("ctx", "exp"), None, None)
    placed = (rows, rows, rows, rows, P(), rows, rows, P(("dp", "exp"), "ctx"), rows, weights, weights)
    body = per_device if mesh.shape["dp"] == 2 and mesh.shape["exp"] == 4 else routed_device
    return jax.shard_map(
        body,
        mesh=mesh,
        in_specs=placed,
        out_specs=(rows, P(("ctx", "exp"), "dp", None), P(("ctx", "exp"), "dp", None)),
        check_vma=False,
    )
```

```python
import math

import jax
import jax.numpy as jnp
from jax import lax
from jax.experimental import pallas as pl
from jax.experimental.pallas import tpu as pltpu
from jax.sharding import PartitionSpec as P

HEAD_DIM = 128
F32 = jnp.float32
BF16 = jnp.bfloat16
VMEM_LIMIT = 56 * 1024 * 1024


VMEM_SPEC = pl.BlockSpec(memory_space=pltpu.VMEM)
SMEM_SPEC = pl.BlockSpec(memory_space=pltpu.SMEM)
NN = (((1,), (0,)), ((), ()))


def on_chip(body, shapes, name, args, scratch=(), scalars=0):
    return pl.pallas_call(
        body,
        out_shape=shapes,
        in_specs=[SMEM_SPEC] * scalars + [VMEM_SPEC] * (len(args) - scalars),
        out_specs=jax.tree.map(lambda _: VMEM_SPEC, shapes),
        scratch_shapes=list(scratch),
        compiler_params=pltpu.CompilerParams(vmem_limit_bytes=VMEM_LIMIT),
        name=name,
    )(*args)


def pack_heads(arrays, ctx):
    tokens, width_all = arrays[0].shape
    width = width_all // ctx

    def body(*refs):
        for i, ref in enumerate(refs[:-1]):
            for j in range(ctx):
                refs[-1][j, i] = ref[:, j * width : (j + 1) * width]

    shape = jax.ShapeDtypeStruct((ctx, len(arrays), tokens, width), BF16)
    return on_chip(body, shape, "pack_heads", arrays)


def attend(packs):
    ctx, _, tokens, width = packs.shape
    scale = 1.0 / math.sqrt(HEAD_DIM)
    nt = (((1,), (1,)), ((), ()))

    def body(packs, out):
        for h in range(width // HEAD_DIM):
            cols = slice(h * HEAD_DIM, (h + 1) * HEAD_DIM)
            q, k, v = (
                jnp.concatenate([packs[j, i, :, cols] for j in range(ctx)], axis=0)
                for i in range(3)
            )
            scores = lax.dot_general(q, k, nt, preferred_element_type=F32) * scale
            largest = jnp.max(scores, axis=1, keepdims=True)
            powers = jnp.exp(scores - largest)
            probs = (powers / jnp.sum(powers, axis=1, keepdims=True)).astype(BF16)
            attended = lax.dot_general(probs, v, NN, preferred_element_type=F32)
            for j in range(ctx):
                rows = slice(j * tokens, (j + 1) * tokens)
                out[rows, cols] = (packs[j, 3, :, cols].astype(F32) + attended[rows]).astype(BF16)

    return on_chip(body, jax.ShapeDtypeStruct((ctx * tokens, width), BF16), "attend", [packs])


def selection(gate, cap):
    tokens = gate.shape[1]
    lower = lax.broadcasted_iota(jnp.int32, (tokens, tokens), 0)
    upper = lax.broadcasted_iota(jnp.int32, (tokens, tokens), 1)
    running = (lower <= upper).astype(BF16)
    row_number = lax.broadcasted_iota(jnp.int32, (cap, tokens), 0).astype(F32)
    picked = gate != 0.0
    marks = jnp.broadcast_to(picked.astype(F32), (8, tokens)).astype(BF16)
    rank = lax.dot_general(marks, running, NN, preferred_element_type=F32)[:1]
    return jnp.logical_and(row_number + 1.0 == rank, picked)


def cot_rows(place, down, blocks, cap, parts):
    seqs, (ctx, rows_in, width_all) = len(blocks), blocks[0].shape
    tokens = rows_in - 8
    half, hidden_width = width_all // parts, down.shape[1]
    count = seqs * ctx * cap

    def body(place, down, *refs):
        inputs, (cot_out, back_out, column_out, gate_out, cot_ref) = refs[:seqs], refs[seqs:]
        column = pl.ds(pl.multiple_of(place[2] * tokens, tokens), tokens)
        for i in range(seqs):
            for t in range(ctx):
                terms = inputs[i][t, tokens : tokens + 8, column].astype(F32)
                gate = terms[0:1] + terms[1:2] + terms[2:3]
                gate_out[i * ctx + t] = gate
                chosen = selection(gate, cap)
                select = chosen.astype(F32).astype(BF16)
                at = (i * ctx + t) * cap
                column_out[at : at + cap, :] = jnp.broadcast_to(
                    jnp.sum(jnp.where(chosen, gate, 0.0), axis=1, keepdims=True), (cap, 128)
                )
                for p in range(parts):
                    block = inputs[i][t, :tokens, p * half : (p + 1) * half]
                    rows = lax.dot_general(select, block, NN, preferred_element_type=F32)
                    cot_ref[p, at : at + cap, :] = rows.astype(BF16)
        back = None
        for p in range(parts):
            term = lax.dot_general(
                cot_ref[p], down[p * half : (p + 1) * half, :], NN, preferred_element_type=F32
            )
            back = term if back is None else back + term
        back_out[...] = back * column_out[:, :1]
        cot_out[...] = cot_ref[place[1]]

    shapes = [
        jax.ShapeDtypeStruct((count, half), BF16),
        jax.ShapeDtypeStruct((count, hidden_width), F32),
        jax.ShapeDtypeStruct((count, 128), F32),
        jax.ShapeDtypeStruct((seqs * ctx, 1, tokens), F32),
    ]
    scratch = [pltpu.VMEM((parts, count, half), BF16)]
    return on_chip(body, shapes, "cot_rows", [place, down, *blocks], scratch, 1)


def stream_rows(place, gain, gate_up, slices, back, columns, gates, cap, parts):
    seqs, (ctx, length, width) = len(slices), slices[0].shape
    tokens, width_all = length // ctx, width * ctx
    half, hidden_width = width_all // parts, back.shape[1]
    count = seqs * ctx * cap

    def body(place, gain, gate_up, back_in, columns, gates, *refs):
        inputs, (norm_out, back_out, hidden_out, rows_ref) = refs[:seqs], refs[seqs:]
        for i in range(seqs):
            for t in range(ctx):
                first = pl.multiple_of(place[3 + t] * tokens, tokens)
                select = selection(gates[i * ctx + t], cap).astype(F32).astype(BF16)
                at = (i * ctx + t) * cap
                for f in range(ctx):
                    block = inputs[i][f, pl.ds(first, tokens), :]
                    rows = lax.dot_general(select, block, NN, preferred_element_type=F32)
                    rows_ref[place[3 + f], at : at + cap, :] = rows.astype(BF16)
        total = None
        for f in range(ctx):
            wide = rows_ref[f].astype(F32)
            square = jnp.sum(wide * wide, axis=1, keepdims=True)
            total = square if total is None else total + square
        factor = lax.rsqrt(total / width_all + 1e-05)
        proj = None
        for f in range(ctx):
            normed = (rows_ref[f].astype(F32) * factor * gain[f]).astype(BF16)
            rows_ref[f] = normed
            term = lax.dot_general(
                normed, gate_up[f * width : (f + 1) * width, :], NN, preferred_element_type=F32
            )
            proj = term if proj is None else proj + term
        gate_part, up_part = proj[:, :hidden_width], proj[:, hidden_width:]
        sigma = 1.0 / (1.0 + jnp.exp(-gate_part))
        activated = gate_part * sigma
        back = back_in[...]
        hidden_out[...] = (activated * up_part * columns[:, :1]).astype(BF16)
        slope = sigma * (1.0 + gate_part * (1.0 - sigma))
        back_out[:, :hidden_width] = (back * up_part * slope).astype(BF16)
        back_out[:, hidden_width:] = (back * activated).astype(BF16)
        each = ctx // parts
        for f in range(each):
            norm_out[:, f * width : (f + 1) * width] = rows_ref[place[1] * each + f]

    shapes = [
        jax.ShapeDtypeStruct((count, half), BF16),
        jax.ShapeDtypeStruct((count, 2 * hidden_width), BF16),
        jax.ShapeDtypeStruct((count, hidden_width), BF16),
    ]
    scratch = [pltpu.VMEM((ctx, count, width), BF16)]
    args = [place, gain, gate_up, back, columns, gates, *slices]
    return on_chip(body, shapes, "stream_rows", args, scratch, 1)


def own_rows(place, slices):
    ctx, length, width = slices.shape
    tokens = length // ctx

    def body(place, slices, out, rows_ref):
        own = pl.ds(pl.multiple_of(place[0] * tokens, tokens), tokens)
        for f in range(ctx):
            rows_ref[place[3 + f]] = slices[f, own, :]
        for f in range(ctx):
            out[:, f * width : (f + 1) * width] = rows_ref[f]

    shape = jax.ShapeDtypeStruct((tokens, ctx * width), BF16)
    scratch = [pltpu.VMEM((ctx, tokens, width), BF16)]
    return on_chip(body, shape, "own_rows", [place, slices], scratch, 1)


def grads_kernel(*refs, groups, add):
    norms, cots, backs, hiddens = (refs[i * groups : (i + 1) * groups] for i in range(4))
    rest = refs[4 * groups :]
    tn = (((0,), (0,)), ((), ()))

    def whole(parts):
        return jnp.concatenate([p[...] for p in parts], axis=0)

    left = lax.dot_general(whole(norms), whole(backs), tn, preferred_element_type=F32)
    right = lax.dot_general(whole(cots), whole(hiddens), tn, preferred_element_type=F32)
    out_left, out_right = rest[-2:]
    if add:
        left = left + rest[0][0]
        right = right + rest[1][0]
    out_left[0] = left
    out_right[0] = right


def grads(pieces, before):
    groups = len(pieces)
    norms, cots, backs, hiddens = zip(*pieces)
    count, half = norms[0].shape
    step = 256
    tall = [pl.BlockSpec((count, step), lambda i: (0, i))] * groups
    out_widths = (backs[0].shape[1], hiddens[0].shape[1])
    full = [
        pl.BlockSpec((count, w), lambda i: (0, 0)) for w in out_widths for _ in range(groups)
    ]
    outs = [pl.BlockSpec((1, step, w), lambda i: (0, i, 0)) for w in out_widths]
    add = before is not None
    args = [*norms, *cots, *backs, *hiddens] + (list(before) if add else [])
    return pl.pallas_call(
        lambda *refs: grads_kernel(*refs, groups=groups, add=add),
        out_shape=[jax.ShapeDtypeStruct((1, half, w), F32) for w in out_widths],
        grid=(half // step,),
        in_specs=tall + tall + full + (outs if add else []),
        out_specs=outs,
        input_output_aliases={4 * groups: 0, 4 * groups + 1: 1} if add else {},
        compiler_params=pltpu.CompilerParams(vmem_limit_bytes=VMEM_LIMIT),
        name="grads",
    )(*args)


def shifted(value, axis, step, count):
    return lax.ppermute(value, axis, [(i, (i + step) % count) for i in range(count)])


def flipped(value, axis, mask, count):
    return lax.ppermute(value, axis, [(i, i ^ mask) for i in range(count)])


def after(value, *others):
    return lax.optimization_barrier((value, *others))[0]


SOURCES = ((0, 1, 2, 3), (1, 0, 1, 2), (2, 2, 3, 1), (3, 3, 0, 0))


def spread(own, z, exp, cut, waits=None, midway=None):
    waits = waits or {}

    def ready(number, values):
        held = lax.optimization_barrier((values, waits.get(number, ())))
        return held[0]

    def up(value, pairs):
        return lax.ppermute(value, "ctx", pairs)

    def x(value):
        return flipped(value, "exp", 2, exp)

    def y(value):
        return flipped(value, "dp", 1, 2)

    def core(value):
        return flipped(value, "exp", 1, exp)

    count = own.shape[0]
    up1, down1 = up(own, [(0, 1), (1, 2), (2, 3)]), up(own, [(1, 0), (2, 1), (3, 2)])
    x0, y0 = x(own), y(own)
    up1, down1, x0, y0 = ready(2, (up1, down1, x0, y0))
    one = jnp.where(z == 0, down1, up1)
    up2, down2 = up(up1, [(1, 2), (2, 3)]), up(down1, [(1, 0), (2, 1)])
    x1 = x(jnp.concatenate([one, y0[cut:]]))
    y1 = y(jnp.concatenate([one, x0[:cut]]))
    up2, down2, x1, y1 = ready(3, (up2, down2, x1, y1))
    two = jnp.where(z == 3, up2, jnp.where(z == 0, down2, down1))
    middle = jnp.where(z == 2, up2, down2)
    ends = up(middle, [(1, 0), (2, 3)])
    x2 = x(jnp.concatenate([two, y1[cut:count]]))
    y2 = y(jnp.concatenate([two, x1[:cut]]))
    ends, x2, y2 = ready(4, (ends, x2, y2))
    three = jnp.where(jnp.logical_or(z == 0, z == 3), ends, middle)
    x3 = x(jnp.concatenate([three, y2[cut:count]]))
    y3 = y(jnp.concatenate([three, x2[:cut]]))
    mine = jnp.stack([own, one, two, three])
    mine_core = core(mine)
    x3, y3 = ready(5, (x3, y3))
    done = midway(mine, mine_core) if midway else ()
    x4, y4 = x(y3[cut:count]), y(x3[:cut])
    over_x = jnp.stack([x0, x1[:count], x2[:count], x3[:count]])
    over_y = jnp.stack([y0, y1[:count], y2[:count], y3[:count]])
    over_x_core, over_y_core = core(over_x), core(over_y)
    both = jnp.stack(
        [
            jnp.concatenate([a[-cut:], b[cut - count :]])
            for a, b in ((y1, x1), (y2, x2), (y3, x3), (y4, x4))
        ]
    )
    both = lax.optimization_barrier((both, done))[0]
    both_core = core(both)
    return {
        (0, 0): (mine, mine_core),
        (0, 1): (over_x, over_x_core),
        (1, 0): (over_y, over_y_core),
        (1, 1): (both, both_core),
    }


def gate_terms(value):
    terms = []
    for _ in range(3):
        term = lax.reduce_precision(value, 8, 7)
        terms.append(term.astype(BF16))
        value = value - term
    return terms


def expert_gates(routes, gates, flags, experts):
    named = routes[:, :, None] == jnp.arange(experts, dtype=jnp.int32)[None, None, :]
    scaled = gates * flags.astype(F32)[:, None]
    return jnp.sum(jnp.where(named, scaled[:, :, None], 0.0), axis=1)


def per_device(
    queries, keys, values, resid, norm_gain, expert_ids, gate_weights, mask_flags, cotangent, w_gate_up, w_down
):
    ctx, exp, parts = (lax.axis_size(a) for a in ("ctx", "exp", "dp"))
    z, e, part = (lax.axis_index(a) for a in ("ctx", "exp", "dp"))
    experts = ctx * exp
    _, tokens, width_all = queries.shape
    width = width_all // ctx
    most = min(tokens, tokens * expert_ids.shape[2] * 17 // (16 * experts))
    cap = -(-most // 16) * 16

    packed = pack_heads([queries[0], keys[0], values[0], resid[0]], ctx)
    packs = lax.all_to_all(packed, "ctx", split_axis=0, concat_axis=0, tiled=True)
    own_slice = attend(packs)

    by_expert = expert_gates(expert_ids[0], gate_weights[0], mask_flags[0], experts)
    terms = jnp.stack([t.T.reshape(experts * tokens) for t in gate_terms(by_expert)])
    terms = jnp.pad(terms, ((0, 5), (0, width_all - experts * tokens)))
    block = jnp.concatenate([cotangent[0], terms], axis=0)
    cots = spread(after(block, packed), z, exp, tokens // 2, {5: own_slice})

    sources = [jnp.asarray(row, jnp.int32)[z] for row in SOURCES]
    place = jnp.stack([z, part, z * exp + e, *sources]).astype(jnp.int32)
    gain = norm_gain.reshape(ctx, 1, width)
    order = ((0, 0), (0, 1), (1, 0), (1, 1))
    picked = {where: cot_rows(place, w_down[0], cots[where], cap, parts) for where in order}

    def expert(where, slices):
        rows, back, columns, gates = picked[where]
        normed, both, hidden = stream_rows(
            place, gain, w_gate_up[0], slices, back, columns, gates, cap, parts
        )
        return normed, rows, both, hidden

    pieces = {}

    def midway(mine, mine_core):
        pieces[0, 0] = expert((0, 0), (mine, mine_core))
        return pieces[0, 0]

    waits = {3: picked[0, 0], 4: picked[0, 1], 5: (picked[1, 0], picked[1, 1])}
    streams = spread(own_slice, z, exp, tokens * ctx // 2, waits, midway)
    for where in order[1:]:
        pieces[where] = expert(where, streams[where])
    stream = own_rows(place, streams[0, 0][0])
    first = grads([pieces[0, 0], pieces[0, 1]], None)
    left, right = grads([pieces[1, 0], pieces[1, 1]], first)
    return stream[None], left, right


def routed_device(
    queries, keys, values, resid, norm_gain, expert_ids, gate_weights, mask_flags, cotangent, w_gate_up, w_down
):
    ctx, exp = (lax.axis_size(a) for a in ("ctx", "exp"))
    experts = ctx * exp
    _, tokens, width_all = queries.shape
    top = expert_ids.shape[2]
    capacity = min(tokens, tokens * top * 17 // (16 * experts))
    keys_all = lax.all_gather(keys[0], "ctx", axis=0, tiled=True)
    values_all = lax.all_gather(values[0], "ctx", axis=0, tiled=True)
    heads = width_all // HEAD_DIM
    q, k, v = (a.reshape(-1, heads, HEAD_DIM) for a in (queries[0], keys_all, values_all))
    scores = jnp.einsum("qhd,khd->hqk", q, k, preferred_element_type=F32) / math.sqrt(HEAD_DIM)
    powers = jnp.exp(scores - jnp.max(scores, axis=2, keepdims=True))
    probs = (powers / jnp.sum(powers, axis=2, keepdims=True)).astype(BF16)
    attended = jnp.einsum("hqk,khd->qhd", probs, v, preferred_element_type=F32)
    stream = (resid[0].astype(F32) + attended.reshape(tokens, width_all)).astype(BF16)
    wide = lax.optimization_barrier(stream).astype(F32)
    factor = lax.rsqrt(jnp.mean(wide * wide, axis=-1, keepdims=True) + 1e-05)
    normed = (wide * factor * norm_gain).astype(BF16)

    by_expert = expert_gates(expert_ids[0], gate_weights[0], mask_flags[0], experts)
    picked = by_expert != 0.0
    running = jnp.arange(tokens)[:, None] >= jnp.arange(tokens)[None, :]
    rank = jnp.dot(running.astype(BF16), picked.astype(BF16), preferred_element_type=F32) - 1.0
    slot = jnp.arange(capacity, dtype=F32)[None, :, None]
    chosen = jnp.logical_and(rank.T[:, None, :] == slot, picked.T[:, None, :])
    select = chosen.astype(BF16).reshape(experts * capacity, tokens)
    sent_rows = jnp.dot(select, normed, preferred_element_type=F32).astype(BF16)
    gate_rows = jnp.sum(jnp.where(chosen, by_expert.T[:, None, :], 0.0), axis=2).reshape(-1, 1)
    picked_cot = jnp.dot(select, cotangent[0], preferred_element_type=F32)
    sent_grads = (picked_cot * gate_rows).astype(BF16)

    def exchanged(rows):
        rows = rows.reshape(experts, capacity, width_all)
        got = lax.all_to_all(rows, ("ctx", "exp"), split_axis=0, concat_axis=0, tiled=True)
        return got.reshape(-1, width_all)

    input_rows, grad_rows = exchanged(sent_rows), exchanged(sent_grads)
    hidden_width = w_down.shape[2]
    proj = jnp.dot(input_rows, w_gate_up[0], preferred_element_type=F32)
    gate_part, up_part = proj[:, :hidden_width], proj[:, hidden_width:]
    sigma = jax.nn.sigmoid(gate_part)
    activated = gate_part * sigma
    hidden = (activated * up_part).astype(BF16)
    back = jnp.dot(grad_rows, w_down[0], preferred_element_type=F32)
    slope = sigma * (1.0 + gate_part * (1.0 - sigma))
    both = jnp.concatenate([back * up_part * slope, back * activated], axis=1).astype(BF16)
    tn = (((0,), (0,)), ((), ()))
    left = lax.dot_general(input_rows, both, tn, preferred_element_type=F32)
    right = lax.dot_general(grad_rows, hidden, tn, preferred_element_type=F32)
    partial = jnp.concatenate([left, right], axis=1).astype(BF16)
    summed = lax.psum_scatter(partial, "dp", scatter_dimension=0, tiled=True).astype(F32)
    return stream[None], summed[None, :, : 2 * hidden_width], summed[None, :, 2 * hidden_width :]


def solution(mesh):
    rows = P(("dp", "exp"), "ctx", None)
    weights = P(("ctx", "exp"), None, None)
    placed = (rows, rows, rows, rows, P(), rows, rows, P(("dp", "exp"), "ctx"), rows, weights, weights)
    blocks = tuple(mesh.shape[a] for a in ("dp", "ctx", "exp"))
    body = per_device if blocks == (2, 4, 4) else routed_device
    return jax.shard_map(
        body,
        mesh=mesh,
        in_specs=placed,
        out_specs=(rows, P(("ctx", "exp"), "dp", None), P(("ctx", "exp"), "dp", None)),
        check_vma=False,
    )
```

```python
import math

import jax
import jax.numpy as jnp
from jax import lax
from jax.experimental import pallas as pl
from jax.experimental.pallas import tpu as pltpu
from jax.sharding import PartitionSpec as P

HEAD_DIM = 128
F32 = jnp.float32
BF16 = jnp.bfloat16


VMEM_SPEC = pl.BlockSpec(memory_space=pltpu.VMEM)
SMEM_SPEC = pl.BlockSpec(memory_space=pltpu.SMEM)
NN = (((1,), (0,)), ((), ()))


def on_chip(body, shapes, name, args, scratch=(), scalars=0, mib=8):
    return pl.pallas_call(
        body,
        out_shape=shapes,
        in_specs=[SMEM_SPEC] * scalars + [VMEM_SPEC] * (len(args) - scalars),
        out_specs=jax.tree.map(lambda _: VMEM_SPEC, shapes),
        scratch_shapes=list(scratch),
        compiler_params=pltpu.CompilerParams(vmem_limit_bytes=mib * 2**20),
        name=name,
    )(*args)


def pack_heads(arrays, ctx):
    tokens, width_all = arrays[0].shape
    width = width_all // ctx

    def body(*refs):
        for i, ref in enumerate(refs[:-1]):
            for j in range(ctx):
                refs[-1][j, i] = ref[:, j * width : (j + 1) * width]

    shape = jax.ShapeDtypeStruct((ctx, len(arrays), tokens, width), BF16)
    return on_chip(body, shape, "pack_heads", arrays)


def attend(packs):
    ctx, _, tokens, width = packs.shape
    scale = 1.0 / math.sqrt(HEAD_DIM)
    nt = (((1,), (1,)), ((), ()))

    def body(packs, out):
        for h in range(width // HEAD_DIM):
            cols = slice(h * HEAD_DIM, (h + 1) * HEAD_DIM)
            q, k, v = (
                jnp.concatenate([packs[j, i, :, cols] for j in range(ctx)], axis=0)
                for i in range(3)
            )
            scores = lax.dot_general(q, k, nt, preferred_element_type=F32) * scale
            largest = jnp.max(scores, axis=1, keepdims=True)
            powers = jnp.exp(scores - largest)
            probs = (powers / jnp.sum(powers, axis=1, keepdims=True)).astype(BF16)
            attended = lax.dot_general(probs, v, NN, preferred_element_type=F32)
            for j in range(ctx):
                rows = slice(j * tokens, (j + 1) * tokens)
                out[rows, cols] = (packs[j, 3, :, cols].astype(F32) + attended[rows]).astype(BF16)

    return on_chip(body, jax.ShapeDtypeStruct((ctx * tokens, width), BF16), "attend", [packs])


def selection(gate, cap):
    tokens = gate.shape[1]
    lower = lax.broadcasted_iota(jnp.int32, (tokens, tokens), 0)
    upper = lax.broadcasted_iota(jnp.int32, (tokens, tokens), 1)
    running = (lower <= upper).astype(BF16)
    row_number = lax.broadcasted_iota(jnp.int32, (cap, tokens), 0).astype(F32)
    picked = gate != 0.0
    marks = jnp.broadcast_to(picked.astype(F32), (8, tokens)).astype(BF16)
    rank = lax.dot_general(marks, running, NN, preferred_element_type=F32)[:1]
    return jnp.logical_and(row_number + 1.0 == rank, picked)


def cot_rows(place, down, blocks, cap, parts):
    seqs, (ctx, rows_in, width_all) = len(blocks), blocks[0].shape
    tokens = rows_in - 8
    half, hidden_width = width_all // parts, down.shape[1]
    count = seqs * ctx * cap

    def body(place, down, *refs):
        inputs, (cot_out, back_out, column_out, gate_out, cot_ref) = refs[:seqs], refs[seqs:]
        column = pl.ds(pl.multiple_of(place[2] * tokens, tokens), tokens)
        for i in range(seqs):
            for t in range(ctx):
                terms = inputs[i][t, tokens : tokens + 8, column].astype(F32)
                gate = terms[0:1] + terms[1:2] + terms[2:3]
                gate_out[i * ctx + t] = gate
                chosen = selection(gate, cap)
                select = chosen.astype(F32).astype(BF16)
                at = (i * ctx + t) * cap
                column_out[at : at + cap, :] = jnp.broadcast_to(
                    jnp.sum(jnp.where(chosen, gate, 0.0), axis=1, keepdims=True), (cap, 128)
                )
                for p in range(parts):
                    block = inputs[i][t, :tokens, p * half : (p + 1) * half]
                    rows = lax.dot_general(select, block, NN, preferred_element_type=F32)
                    cot_ref[p, at : at + cap, :] = rows.astype(BF16)
        back = None
        for p in range(parts):
            term = lax.dot_general(
                cot_ref[p], down[p * half : (p + 1) * half, :], NN, preferred_element_type=F32
            )
            back = term if back is None else back + term
        back_out[...] = back * column_out[:, :1]
        cot_out[...] = cot_ref[place[1]]

    shapes = [
        jax.ShapeDtypeStruct((count, half), BF16),
        jax.ShapeDtypeStruct((count, hidden_width), F32),
        jax.ShapeDtypeStruct((count, 128), F32),
        jax.ShapeDtypeStruct((seqs * ctx, 1, tokens), F32),
    ]
    scratch = [pltpu.VMEM((parts, count, half), BF16)]
    return on_chip(body, shapes, "cot_rows", [place, down, *blocks], scratch, 1, 16)


def stream_rows(place, gain, gate_up, slices, back, columns, gates, cap, parts, with_own):
    seqs, (ctx, length, width) = len(slices), slices[0].shape
    tokens, width_all = length // ctx, width * ctx
    half, hidden_width = width_all // parts, back.shape[1]
    count = seqs * ctx * cap

    def body(place, gain, gate_up, back_in, columns, gates, *refs):
        inputs, (norm_out, back_out, hidden_out, *own_out, rows_ref) = refs[:seqs], refs[seqs:]
        if with_own:
            own = pl.ds(pl.multiple_of(place[0] * tokens, tokens), tokens)
            for f in range(ctx):
                rows_ref[place[3 + f], :tokens, :] = inputs[0][f, own, :]
            for f in range(ctx):
                own_out[0][:, f * width : (f + 1) * width] = rows_ref[f, :tokens, :]
        for i in range(seqs):
            for t in range(ctx):
                first = pl.multiple_of(place[3 + t] * tokens, tokens)
                select = selection(gates[i * ctx + t], cap).astype(F32).astype(BF16)
                at = (i * ctx + t) * cap
                for f in range(ctx):
                    block = inputs[i][f, pl.ds(first, tokens), :]
                    rows = lax.dot_general(select, block, NN, preferred_element_type=F32)
                    rows_ref[place[3 + f], at : at + cap, :] = rows.astype(BF16)
        total = None
        for f in range(ctx):
            wide = rows_ref[f].astype(F32)
            square = jnp.sum(wide * wide, axis=1, keepdims=True)
            total = square if total is None else total + square
        factor = lax.rsqrt(total / width_all + 1e-05)
        proj = None
        for f in range(ctx):
            normed = (rows_ref[f].astype(F32) * factor * gain[f]).astype(BF16)
            rows_ref[f] = normed
            term = lax.dot_general(
                normed, gate_up[f * width : (f + 1) * width, :], NN, preferred_element_type=F32
            )
            proj = term if proj is None else proj + term
        gate_part, up_part = proj[:, :hidden_width], proj[:, hidden_width:]
        sigma = 1.0 / (1.0 + jnp.exp(-gate_part))
        activated = gate_part * sigma
        back = back_in[...]
        hidden_out[...] = (activated * up_part * columns[:, :1]).astype(BF16)
        slope = sigma * (1.0 + gate_part * (1.0 - sigma))
        back_out[:, :hidden_width] = (back * up_part * slope).astype(BF16)
        back_out[:, hidden_width:] = (back * activated).astype(BF16)
        each = ctx // parts
        for f in range(each):
            norm_out[:, f * width : (f + 1) * width] = rows_ref[place[1] * each + f]

    shapes = [
        jax.ShapeDtypeStruct((count, half), BF16),
        jax.ShapeDtypeStruct((count, 2 * hidden_width), BF16),
        jax.ShapeDtypeStruct((count, hidden_width), BF16),
    ]
    if with_own:
        shapes.append(jax.ShapeDtypeStruct((tokens, width_all), BF16))
    scratch = [pltpu.VMEM((ctx, count, width), BF16)]
    args = [place, gain, gate_up, back, columns, gates, *slices]
    return on_chip(body, shapes, "stream_rows", args, scratch, 1, 26)


def grads_kernel(*refs, groups, add):
    norms, cots, backs, hiddens = (refs[i * groups : (i + 1) * groups] for i in range(4))
    rest = refs[4 * groups :]
    tn = (((0,), (0,)), ((), ()))

    def whole(parts):
        return jnp.concatenate([p[...] for p in parts], axis=0)

    left = lax.dot_general(whole(norms), whole(backs), tn, preferred_element_type=F32)
    right = lax.dot_general(whole(cots), whole(hiddens), tn, preferred_element_type=F32)
    out_left, out_right = rest[-2:]
    if add:
        left = left + rest[0][0]
        right = right + rest[1][0]
    out_left[0] = left
    out_right[0] = right


def grads(pieces, before):
    groups = len(pieces)
    norms, cots, backs, hiddens = zip(*pieces)
    count, half = norms[0].shape
    step = 256
    tall = [pl.BlockSpec((count, step), lambda i: (0, i))] * groups
    out_widths = (backs[0].shape[1], hiddens[0].shape[1])
    full = [
        pl.BlockSpec((count, w), lambda i: (0, 0)) for w in out_widths for _ in range(groups)
    ]
    outs = [pl.BlockSpec((1, step, w), lambda i: (0, i, 0)) for w in out_widths]
    add = before is not None
    args = [*norms, *cots, *backs, *hiddens] + (list(before) if add else [])
    return pl.pallas_call(
        lambda *refs: grads_kernel(*refs, groups=groups, add=add),
        out_shape=[jax.ShapeDtypeStruct((1, half, w), F32) for w in out_widths],
        grid=(half // step,),
        in_specs=tall + tall + full + (outs if add else []),
        out_specs=outs,
        input_output_aliases={4 * groups: 0, 4 * groups + 1: 1} if add else {},
        compiler_params=pltpu.CompilerParams(vmem_limit_bytes=18 * 2**20),
        name="grads",
    )(*args)


def shifted(value, axis, step, count):
    return lax.ppermute(value, axis, [(i, (i + step) % count) for i in range(count)])


def flipped(value, axis, mask, count):
    return lax.ppermute(value, axis, [(i, i ^ mask) for i in range(count)])


def after(value, *others):
    return lax.optimization_barrier((value, *others))[0]


SOURCES = ((0, 1, 2, 3), (1, 0, 1, 2), (2, 2, 3, 1), (3, 3, 0, 0))


def spread(own, z, exp, waits=None, midway=None):
    waits = waits or {}

    def ready(number, values):
        return lax.optimization_barrier((values, waits.get(number, ())))[0]

    def line(value, pairs):
        return lax.ppermute(value, "ctx", pairs)

    def x(value):
        return flipped(value, "exp", 2, exp)

    def y(value):
        return flipped(value, "dp", 1, 2)

    def core(value):
        return flipped(value, "exp", 1, exp)

    up1, down1 = line(own, [(0, 1), (1, 2), (2, 3)]), line(own, [(1, 0), (2, 1), (3, 2)])
    x0, y0 = x(own), y(own)
    up1, down1, x0, y0 = ready(2, (up1, down1, x0, y0))
    one = jnp.where(z == 0, down1, up1)
    up2, down2 = line(up1, [(1, 2), (2, 3)]), line(down1, [(1, 0), (2, 1)])
    x1, y1 = x(one), y(one)
    up2, down2, x1, y1, y0 = ready(3, (up2, down2, x1, y1, y0))
    two = jnp.where(z == 3, up2, jnp.where(z == 0, down2, down1))
    middle = jnp.where(z == 2, up2, down2)
    ends = line(middle, [(1, 0), (2, 3)])
    x2, y2 = x(two), y(two)
    d0, d1 = x(y0), y(x1)
    ends, x2, y2, d0, d1 = ready(4, (ends, x2, y2, d0, d1))
    three = jnp.where(jnp.logical_or(z == 0, z == 3), ends, middle)
    x3, y3 = x(three), y(three)
    mine = jnp.stack([own, one, two, three])
    mine_core = core(mine)
    x3, y3, mine_core, y2 = ready(5, (x3, y3, mine_core, y2))
    d2, d3 = x(y2), y(x3)
    done = midway(mine, mine_core) if midway else ()
    over_x, over_y = jnp.stack([x0, x1, x2, x3]), jnp.stack([y0, y1, y2, y3])
    over_x_core, over_y_core = core(over_x), core(over_y)
    both = lax.optimization_barrier((jnp.stack([d0, d1, d2, d3]), done))[0]
    both_core = core(both)
    return {
        (0, 0): (mine, mine_core),
        (0, 1): (over_x, over_x_core),
        (1, 0): (over_y, over_y_core),
        (1, 1): (both, both_core),
    }, (up2, down2)


def gate_terms(value):
    terms = []
    for _ in range(3):
        term = lax.reduce_precision(value, 8, 7)
        terms.append(term.astype(BF16))
        value = value - term
    return terms


def expert_gates(routes, gates, flags, experts):
    named = routes[:, :, None] == jnp.arange(experts, dtype=jnp.int32)[None, None, :]
    scaled = gates * flags.astype(F32)[:, None]
    return jnp.sum(jnp.where(named, scaled[:, :, None], 0.0), axis=1)


def per_device(
    queries, keys, values, resid, norm_gain, expert_ids, gate_weights, mask_flags, cotangent, w_gate_up, w_down
):
    ctx, exp, parts = (lax.axis_size(a) for a in ("ctx", "exp", "dp"))
    z, e, part = (lax.axis_index(a) for a in ("ctx", "exp", "dp"))
    experts = ctx * exp
    _, tokens, width_all = queries.shape
    width = width_all // ctx
    most = min(tokens, tokens * expert_ids.shape[2] * 17 // (16 * experts))
    cap = -(-most // 16) * 16

    by_expert = expert_gates(expert_ids[0], gate_weights[0], mask_flags[0], experts)
    terms = jnp.stack([t.T.reshape(experts * tokens) for t in gate_terms(by_expert)])
    terms = jnp.pad(terms, ((0, 5), (0, width_all - experts * tokens)))
    block = jnp.concatenate([cotangent[0], terms], axis=0)
    cots, line_done = spread(block, z, exp)

    packed = pack_heads([queries[0], keys[0], values[0], resid[0]], ctx)
    packed = after(packed, line_done)
    packs = lax.all_to_all(packed, "ctx", split_axis=0, concat_axis=0, tiled=True)
    own_slice = attend(packs)

    sources = [jnp.asarray(row, jnp.int32)[z] for row in SOURCES]
    place = jnp.stack([z, part, z * exp + e, *sources]).astype(jnp.int32)
    gain = norm_gain.reshape(ctx, 1, width)
    order = ((0, 0), (0, 1), (1, 0), (1, 1))
    picked = {where: cot_rows(place, w_down[0], cots[where], cap, parts) for where in order}

    def expert(where, slices):
        rows, back, columns, gates = picked[where]
        normed, both, hidden, *own = stream_rows(
            place, gain, w_gate_up[0], slices, back, columns, gates, cap, parts, where == (0, 0)
        )
        return normed, rows, both, hidden, *own

    pieces = {}

    def midway(mine, mine_core):
        pieces[0, 0] = expert((0, 0), (mine, mine_core))
        return pieces[0, 0]

    waits = {3: picked[0, 0], 4: picked[0, 1], 5: (picked[1, 0], picked[1, 1])}
    streams, _ = spread(own_slice, z, exp, waits, midway)
    for where in order[1:]:
        pieces[where] = expert(where, streams[where])
    stream = pieces[0, 0][4]
    first = grads([pieces[0, 0][:4], pieces[0, 1]], None)
    left, right = grads([pieces[1, 0], pieces[1, 1]], first)
    return stream[None], left, right


def routed_device(
    queries, keys, values, resid, norm_gain, expert_ids, gate_weights, mask_flags, cotangent, w_gate_up, w_down
):
    ctx, exp = (lax.axis_size(a) for a in ("ctx", "exp"))
    experts = ctx * exp
    _, tokens, width_all = queries.shape
    top = expert_ids.shape[2]
    capacity = min(tokens, tokens * top * 17 // (16 * experts))
    keys_all = lax.all_gather(keys[0], "ctx", axis=0, tiled=True)
    values_all = lax.all_gather(values[0], "ctx", axis=0, tiled=True)
    heads = width_all // HEAD_DIM
    q, k, v = (a.reshape(-1, heads, HEAD_DIM) for a in (queries[0], keys_all, values_all))
    scores = jnp.einsum("qhd,khd->hqk", q, k, preferred_element_type=F32) / math.sqrt(HEAD_DIM)
    powers = jnp.exp(scores - jnp.max(scores, axis=2, keepdims=True))
    probs = (powers / jnp.sum(powers, axis=2, keepdims=True)).astype(BF16)
    attended = jnp.einsum("hqk,khd->qhd", probs, v, preferred_element_type=F32)
    stream = (resid[0].astype(F32) + attended.reshape(tokens, width_all)).astype(BF16)
    wide = lax.optimization_barrier(stream).astype(F32)
    factor = lax.rsqrt(jnp.mean(wide * wide, axis=-1, keepdims=True) + 1e-05)
    normed = (wide * factor * norm_gain).astype(BF16)

    by_expert = expert_gates(expert_ids[0], gate_weights[0], mask_flags[0], experts)
    picked = by_expert != 0.0
    running = jnp.arange(tokens)[:, None] >= jnp.arange(tokens)[None, :]
    rank = jnp.dot(running.astype(BF16), picked.astype(BF16), preferred_element_type=F32) - 1.0
    slot = jnp.arange(capacity, dtype=F32)[None, :, None]
    chosen = jnp.logical_and(rank.T[:, None, :] == slot, picked.T[:, None, :])
    select = chosen.astype(BF16).reshape(experts * capacity, tokens)
    sent_rows = jnp.dot(select, normed, preferred_element_type=F32).astype(BF16)
    gate_rows = jnp.sum(jnp.where(chosen, by_expert.T[:, None, :], 0.0), axis=2).reshape(-1, 1)
    picked_cot = jnp.dot(select, cotangent[0], preferred_element_type=F32)
    sent_grads = (picked_cot * gate_rows).astype(BF16)

    def exchanged(rows):
        rows = rows.reshape(experts, capacity, width_all)
        got = lax.all_to_all(rows, ("ctx", "exp"), split_axis=0, concat_axis=0, tiled=True)
        return got.reshape(-1, width_all)

    input_rows, grad_rows = exchanged(sent_rows), exchanged(sent_grads)
    hidden_width = w_down.shape[2]
    proj = jnp.dot(input_rows, w_gate_up[0], preferred_element_type=F32)
    gate_part, up_part = proj[:, :hidden_width], proj[:, hidden_width:]
    sigma = jax.nn.sigmoid(gate_part)
    activated = gate_part * sigma
    hidden = (activated * up_part).astype(BF16)
    back = jnp.dot(grad_rows, w_down[0], preferred_element_type=F32)
    slope = sigma * (1.0 + gate_part * (1.0 - sigma))
    both = jnp.concatenate([back * up_part * slope, back * activated], axis=1).astype(BF16)
    tn = (((0,), (0,)), ((), ()))
    left = lax.dot_general(input_rows, both, tn, preferred_element_type=F32)
    right = lax.dot_general(grad_rows, hidden, tn, preferred_element_type=F32)
    partial = jnp.concatenate([left, right], axis=1).astype(BF16)
    summed = lax.psum_scatter(partial, "dp", scatter_dimension=0, tiled=True).astype(F32)
    return stream[None], summed[None, :, : 2 * hidden_width], summed[None, :, 2 * hidden_width :]


def solution(mesh):
    rows = P(("dp", "exp"), "ctx", None)
    weights = P(("ctx", "exp"), None, None)
    placed = (rows, rows, rows, rows, P(), rows, rows, P(("dp", "exp"), "ctx"), rows, weights, weights)
    blocks = tuple(mesh.shape[a] for a in ("dp", "ctx", "exp"))
    body = per_device if blocks == (2, 4, 4) else routed_device
    return jax.shard_map(
        body,
        mesh=mesh,
        in_specs=placed,
        out_specs=(rows, P(("ctx", "exp"), "dp", None), P(("ctx", "exp"), "dp", None)),
        check_vma=False,
    )
```

```python
import math

import jax
import jax.numpy as jnp
from jax import lax
from jax.experimental import pallas as pl
from jax.experimental.pallas import tpu as pltpu
from jax.sharding import PartitionSpec as P

HEAD_DIM = 128
F32 = jnp.float32
BF16 = jnp.bfloat16


VMEM_SPEC = pl.BlockSpec(memory_space=pltpu.VMEM)
SMEM_SPEC = pl.BlockSpec(memory_space=pltpu.SMEM)
NN = (((1,), (0,)), ((), ()))


def on_chip(body, shapes, name, args, scratch=(), scalars=0, mib=8):
    return pl.pallas_call(
        body,
        out_shape=shapes,
        in_specs=[SMEM_SPEC] * scalars + [VMEM_SPEC] * (len(args) - scalars),
        out_specs=jax.tree.map(lambda _: VMEM_SPEC, shapes),
        scratch_shapes=list(scratch),
        compiler_params=pltpu.CompilerParams(vmem_limit_bytes=mib * 2**20),
        name=name,
    )(*args)


def pack_heads(arrays, ctx):
    tokens, width_all = arrays[0].shape
    width = width_all // ctx

    def body(*refs):
        for i, ref in enumerate(refs[:-1]):
            for j in range(ctx):
                refs[-1][j, i] = ref[:, j * width : (j + 1) * width]

    shape = jax.ShapeDtypeStruct((ctx, len(arrays), tokens, width), BF16)
    return on_chip(body, shape, "pack_heads", arrays)


def attend(packs):
    ctx, _, tokens, width = packs.shape
    scale = 1.0 / math.sqrt(HEAD_DIM)
    nt = (((1,), (1,)), ((), ()))

    def body(packs, out):
        for h in range(width // HEAD_DIM):
            cols = slice(h * HEAD_DIM, (h + 1) * HEAD_DIM)
            q, k, v = (
                jnp.concatenate([packs[j, i, :, cols] for j in range(ctx)], axis=0)
                for i in range(3)
            )
            scores = lax.dot_general(q, k, nt, preferred_element_type=F32) * scale
            largest = jnp.max(scores, axis=1, keepdims=True)
            powers = jnp.exp(scores - largest)
            probs = (powers / jnp.sum(powers, axis=1, keepdims=True)).astype(BF16)
            attended = lax.dot_general(probs, v, NN, preferred_element_type=F32)
            for j in range(ctx):
                rows = slice(j * tokens, (j + 1) * tokens)
                out[rows, cols] = (packs[j, 3, :, cols].astype(F32) + attended[rows]).astype(BF16)

    return on_chip(body, jax.ShapeDtypeStruct((ctx * tokens, width), BF16), "attend", [packs])


def selection(gate, cap):
    tokens = gate.shape[1]
    lower = lax.broadcasted_iota(jnp.int32, (tokens, tokens), 0)
    upper = lax.broadcasted_iota(jnp.int32, (tokens, tokens), 1)
    running = (lower <= upper).astype(BF16)
    row_number = lax.broadcasted_iota(jnp.int32, (cap, tokens), 0).astype(F32)
    picked = gate != 0.0
    marks = jnp.broadcast_to(picked.astype(F32), (8, tokens)).astype(BF16)
    rank = lax.dot_general(marks, running, NN, preferred_element_type=F32)[:1]
    return jnp.logical_and(row_number + 1.0 == rank, picked)


def pairs_of(ctx):
    return [tuple(range(t, min(t + 2, ctx))) for t in range(0, ctx, 2)]


def diagonal(chosen):
    ones = [c.astype(F32) for c in chosen]
    rows = [
        jnp.concatenate([o if i == j else jnp.zeros_like(o) for j in range(len(ones))], axis=1)
        for i, o in enumerate(ones)
    ]
    return jnp.concatenate(rows, axis=0).astype(BF16)


def cot_rows(place, down, blocks, cap, parts):
    seqs, (ctx, rows_in, width_all) = len(blocks), blocks[0].shape
    tokens = rows_in - 8
    half, hidden_width = width_all // parts, down.shape[1]
    count = seqs * ctx * cap

    def body(place, down, *refs):
        inputs, (cot_out, back_out, column_out, gate_out, cot_ref) = refs[:seqs], refs[seqs:]
        column = pl.ds(pl.multiple_of(place[2] * tokens, tokens), tokens)
        for i in range(seqs):
            for pair in pairs_of(ctx):
                at = (i * ctx + pair[0]) * cap
                chosen = []
                for k, t in enumerate(pair):
                    terms = inputs[i][t, tokens : tokens + 8, column].astype(F32)
                    gate = terms[0:1] + terms[1:2] + terms[2:3]
                    gate_out[i * ctx + t] = gate
                    chosen.append(selection(gate, cap))
                    column_out[at + k * cap : at + (k + 1) * cap, :] = jnp.broadcast_to(
                        jnp.sum(jnp.where(chosen[k], gate, 0.0), axis=1, keepdims=True), (cap, 128)
                    )
                select = diagonal(chosen)
                for p in range(parts):
                    block = jnp.concatenate(
                        [inputs[i][t, :tokens, p * half : (p + 1) * half] for t in pair], axis=0
                    )
                    rows = lax.dot_general(select, block, NN, preferred_element_type=F32)
                    cot_ref[p, at : at + len(pair) * cap, :] = rows.astype(BF16)
        back = None
        for p in range(parts):
            term = lax.dot_general(
                cot_ref[p], down[p * half : (p + 1) * half, :], NN, preferred_element_type=F32
            )
            back = term if back is None else back + term
        back_out[...] = back * column_out[:, :1]
        cot_out[...] = cot_ref[place[1]]

    shapes = [
        jax.ShapeDtypeStruct((count, half), BF16),
        jax.ShapeDtypeStruct((count, hidden_width), F32),
        jax.ShapeDtypeStruct((count, 128), F32),
        jax.ShapeDtypeStruct((seqs * ctx, 1, tokens), F32),
    ]
    scratch = [pltpu.VMEM((parts, count, half), BF16)]
    return on_chip(body, shapes, "cot_rows", [place, down, *blocks], scratch, 1, 16)


def stream_rows(place, gain, gate_up, slices, back, columns, gates, cap, parts, with_own):
    seqs, (ctx, length, width) = len(slices), slices[0].shape
    tokens, width_all = length // ctx, width * ctx
    half, hidden_width = width_all // parts, back.shape[1]
    count = seqs * ctx * cap

    def body(place, gain, gate_up, back_in, columns, gates, *refs):
        inputs, (norm_out, back_out, hidden_out, *own_out, rows_ref) = refs[:seqs], refs[seqs:]
        if with_own:
            own = pl.ds(pl.multiple_of(place[0] * tokens, tokens), tokens)
            for f in range(ctx):
                rows_ref[place[3 + f], :tokens, :] = inputs[0][f, own, :]
            for f in range(ctx):
                own_out[0][:, f * width : (f + 1) * width] = rows_ref[f, :tokens, :]
        for i in range(seqs):
            for pair in pairs_of(ctx):
                firsts = [pl.multiple_of(place[3 + t] * tokens, tokens) for t in pair]
                select = diagonal([selection(gates[i * ctx + t], cap) for t in pair])
                at = (i * ctx + pair[0]) * cap
                for f in range(ctx):
                    block = jnp.concatenate(
                        [inputs[i][f, pl.ds(first, tokens), :] for first in firsts], axis=0
                    )
                    rows = lax.dot_general(select, block, NN, preferred_element_type=F32)
                    rows_ref[place[3 + f], at : at + len(pair) * cap, :] = rows.astype(BF16)
        total = None
        for f in range(ctx):
            wide = rows_ref[f].astype(F32)
            square = jnp.sum(wide * wide, axis=1, keepdims=True)
            total = square if total is None else total + square
        factor = lax.rsqrt(total / width_all + 1e-05)
        proj = None
        for f in range(ctx):
            normed = (rows_ref[f].astype(F32) * factor * gain[f]).astype(BF16)
            rows_ref[f] = normed
            term = lax.dot_general(
                normed, gate_up[f * width : (f + 1) * width, :], NN, preferred_element_type=F32
            )
            proj = term if proj is None else proj + term
        gate_part, up_part = proj[:, :hidden_width], proj[:, hidden_width:]
        sigma = 1.0 / (1.0 + jnp.exp(-gate_part))
        activated = gate_part * sigma
        back = back_in[...]
        hidden_out[...] = (activated * up_part * columns[:, :1]).astype(BF16)
        slope = sigma * (1.0 + gate_part * (1.0 - sigma))
        back_out[:, :hidden_width] = (back * up_part * slope).astype(BF16)
        back_out[:, hidden_width:] = (back * activated).astype(BF16)
        each = ctx // parts
        for f in range(each):
            norm_out[:, f * width : (f + 1) * width] = rows_ref[place[1] * each + f]

    shapes = [
        jax.ShapeDtypeStruct((count, half), BF16),
        jax.ShapeDtypeStruct((count, 2 * hidden_width), BF16),
        jax.ShapeDtypeStruct((count, hidden_width), BF16),
    ]
    if with_own:
        shapes.append(jax.ShapeDtypeStruct((tokens, width_all), BF16))
    scratch = [pltpu.VMEM((ctx, count, width), BF16)]
    args = [place, gain, gate_up, back, columns, gates, *slices]
    return on_chip(body, shapes, "stream_rows", args, scratch, 1, 26)


def grads_kernel(*refs, groups):
    norms, cots, backs, hiddens = (refs[i * groups : (i + 1) * groups] for i in range(4))
    out_left, out_right = refs[4 * groups :]
    tn = (((0,), (0,)), ((), ()))

    def whole(parts):
        return jnp.concatenate([p[...] for p in parts], axis=0)

    out_left[0] = lax.dot_general(whole(norms), whole(backs), tn, preferred_element_type=F32)
    out_right[0] = lax.dot_general(whole(cots), whole(hiddens), tn, preferred_element_type=F32)


def grads(pieces):
    groups = len(pieces)
    norms, cots, backs, hiddens = zip(*pieces)
    count, half = norms[0].shape
    step = min(half, 512)
    tall = [pl.BlockSpec((count, step), lambda i: (0, i))] * groups
    out_widths = (backs[0].shape[1], hiddens[0].shape[1])
    full = [
        pl.BlockSpec((count, w), lambda i: (0, 0)) for w in out_widths for _ in range(groups)
    ]
    return pl.pallas_call(
        lambda *refs: grads_kernel(*refs, groups=groups),
        out_shape=[jax.ShapeDtypeStruct((1, half, w), F32) for w in out_widths],
        grid=(half // step,),
        in_specs=tall + tall + full,
        out_specs=[pl.BlockSpec((1, step, w), lambda i: (0, i, 0)) for w in out_widths],
        compiler_params=pltpu.CompilerParams(vmem_limit_bytes=32 * 2**20),
        name="grads",
    )(*norms, *cots, *backs, *hiddens)


def shifted(value, axis, step, count):
    return lax.ppermute(value, axis, [(i, (i + step) % count) for i in range(count)])


def flipped(value, axis, mask, count):
    return lax.ppermute(value, axis, [(i, i ^ mask) for i in range(count)])


def after(value, *others):
    return lax.optimization_barrier((value, *others))[0]


SOURCES = ((0, 1, 2, 3), (1, 0, 1, 2), (2, 2, 3, 1), (3, 3, 0, 0))


def spread(own, z, exp, waits=None, midway=None):
    waits = waits or {}

    def ready(number, values):
        return lax.optimization_barrier((values, waits.get(number, ())))[0]

    def line(value, pairs):
        return lax.ppermute(value, "ctx", pairs)

    def x(value):
        return flipped(value, "exp", 2, exp)

    def y(value):
        return flipped(value, "dp", 1, 2)

    def core(value):
        return flipped(value, "exp", 1, exp)

    up1, down1 = line(own, [(0, 1), (1, 2), (2, 3)]), line(own, [(1, 0), (2, 1), (3, 2)])
    x0, y0 = x(own), y(own)
    up1, down1, x0, y0 = ready(2, (up1, down1, x0, y0))
    one = jnp.where(z == 0, down1, up1)
    up2, down2 = line(up1, [(1, 2), (2, 3)]), line(down1, [(1, 0), (2, 1)])
    x1, y1 = x(one), y(one)
    up2, down2, x1, y1, y0 = ready(3, (up2, down2, x1, y1, y0))
    two = jnp.where(z == 3, up2, jnp.where(z == 0, down2, down1))
    middle = jnp.where(z == 2, up2, down2)
    ends = line(middle, [(1, 0), (2, 3)])
    x2, y2 = x(two), y(two)
    d0, d1 = x(y0), y(x1)
    ends, x2, y2, d0, d1 = ready(4, (ends, x2, y2, d0, d1))
    three = jnp.where(jnp.logical_or(z == 0, z == 3), ends, middle)
    x3, y3 = x(three), y(three)
    mine = jnp.stack([own, one, two, three])
    mine_core = core(mine)
    x3, y3, mine_core, y2 = ready(5, (x3, y3, mine_core, y2))
    d2, d3 = x(y2), y(x3)
    done = midway(mine, mine_core) if midway else ()
    over_x, over_y = jnp.stack([x0, x1, x2, x3]), jnp.stack([y0, y1, y2, y3])
    over_x_core, over_y_core = core(over_x), core(over_y)
    both = lax.optimization_barrier((jnp.stack([d0, d1, d2, d3]), done))[0]
    both_core = core(both)
    return {
        (0, 0): (mine, mine_core),
        (0, 1): (over_x, over_x_core),
        (1, 0): (over_y, over_y_core),
        (1, 1): (both, both_core),
    }, (up2, down2)


def gate_terms(value):
    terms = []
    for _ in range(3):
        term = lax.reduce_precision(value, 8, 7)
        terms.append(term.astype(BF16))
        value = value - term
    return terms


def expert_gates(routes, gates, flags, experts):
    named = routes[:, :, None] == jnp.arange(experts, dtype=jnp.int32)[None, None, :]
    scaled = gates * flags.astype(F32)[:, None]
    return jnp.sum(jnp.where(named, scaled[:, :, None], 0.0), axis=1)


def per_device(
    queries, keys, values, resid, norm_gain, expert_ids, gate_weights, mask_flags, cotangent, w_gate_up, w_down
):
    ctx, exp, parts = (lax.axis_size(a) for a in ("ctx", "exp", "dp"))
    z, e, part = (lax.axis_index(a) for a in ("ctx", "exp", "dp"))
    experts = ctx * exp
    _, tokens, width_all = queries.shape
    width = width_all // ctx
    most = min(tokens, tokens * expert_ids.shape[2] * 17 // (16 * experts))
    cap = -(-most // 8) * 8

    by_expert = expert_gates(expert_ids[0], gate_weights[0], mask_flags[0], experts)
    terms = jnp.stack([t.T.reshape(experts * tokens) for t in gate_terms(by_expert)])
    terms = jnp.pad(terms, ((0, 5), (0, width_all - experts * tokens)))
    block = jnp.concatenate([cotangent[0], terms], axis=0)
    sources = [jnp.asarray(row, jnp.int32)[z] for row in SOURCES]
    place = jnp.stack([z, part, z * exp + e, *sources]).astype(jnp.int32)
    packed = pack_heads([queries[0], keys[0], values[0], resid[0]], ctx)
    cots, line_done = spread(block, z, exp, {3: (packed, place)})

    packed = after(packed, line_done)
    packs = lax.all_to_all(packed, "ctx", split_axis=0, concat_axis=0, tiled=True)
    own_slice = attend(packs)

    gain = norm_gain.reshape(ctx, 1, width)
    order = ((0, 0), (0, 1), (1, 0), (1, 1))
    picked = {where: cot_rows(place, w_down[0], cots[where], cap, parts) for where in order}

    def expert(where, slices):
        rows, back, columns, gates = picked[where]
        normed, both, hidden, *own = stream_rows(
            place, gain, w_gate_up[0], slices, back, columns, gates, cap, parts, where == (0, 0)
        )
        return normed, rows, both, hidden, *own

    pieces = {}

    def midway(mine, mine_core):
        pieces[0, 0] = expert((0, 0), (mine, mine_core))
        return pieces[0, 0]

    waits = {2: picked[0, 0], 4: picked[0, 1], 5: (picked[1, 0], picked[1, 1])}
    streams, _ = spread(own_slice, z, exp, waits, midway)
    for where in order[1:]:
        pieces[where] = expert(where, streams[where])
    stream = pieces[0, 0][4]
    left, right = grads([pieces[where][:4] for where in order])
    return stream[None], left, right


def routed_device(
    queries, keys, values, resid, norm_gain, expert_ids, gate_weights, mask_flags, cotangent, w_gate_up, w_down
):
    ctx, exp = (lax.axis_size(a) for a in ("ctx", "exp"))
    experts = ctx * exp
    _, tokens, width_all = queries.shape
    top = expert_ids.shape[2]
    capacity = min(tokens, tokens * top * 17 // (16 * experts))
    keys_all = lax.all_gather(keys[0], "ctx", axis=0, tiled=True)
    values_all = lax.all_gather(values[0], "ctx", axis=0, tiled=True)
    heads = width_all // HEAD_DIM
    q, k, v = (a.reshape(-1, heads, HEAD_DIM) for a in (queries[0], keys_all, values_all))
    scores = jnp.einsum("qhd,khd->hqk", q, k, preferred_element_type=F32) / math.sqrt(HEAD_DIM)
    powers = jnp.exp(scores - jnp.max(scores, axis=2, keepdims=True))
    probs = (powers / jnp.sum(powers, axis=2, keepdims=True)).astype(BF16)
    attended = jnp.einsum("hqk,khd->qhd", probs, v, preferred_element_type=F32)
    stream = (resid[0].astype(F32) + attended.reshape(tokens, width_all)).astype(BF16)
    wide = lax.optimization_barrier(stream).astype(F32)
    factor = lax.rsqrt(jnp.mean(wide * wide, axis=-1, keepdims=True) + 1e-05)
    normed = (wide * factor * norm_gain).astype(BF16)

    by_expert = expert_gates(expert_ids[0], gate_weights[0], mask_flags[0], experts)
    picked = by_expert != 0.0
    running = jnp.arange(tokens)[:, None] >= jnp.arange(tokens)[None, :]
    rank = jnp.dot(running.astype(BF16), picked.astype(BF16), preferred_element_type=F32) - 1.0
    slot = jnp.arange(capacity, dtype=F32)[None, :, None]
    chosen = jnp.logical_and(rank.T[:, None, :] == slot, picked.T[:, None, :])
    select = chosen.astype(BF16).reshape(experts * capacity, tokens)
    sent_rows = jnp.dot(select, normed, preferred_element_type=F32).astype(BF16)
    gate_rows = jnp.sum(jnp.where(chosen, by_expert.T[:, None, :], 0.0), axis=2).reshape(-1, 1)
    picked_cot = jnp.dot(select, cotangent[0], preferred_element_type=F32)
    sent_grads = (picked_cot * gate_rows).astype(BF16)

    def exchanged(rows):
        rows = rows.reshape(experts, capacity, width_all)
        got = lax.all_to_all(rows, ("ctx", "exp"), split_axis=0, concat_axis=0, tiled=True)
        return got.reshape(-1, width_all)

    input_rows, grad_rows = exchanged(sent_rows), exchanged(sent_grads)
    hidden_width = w_down.shape[2]
    proj = jnp.dot(input_rows, w_gate_up[0], preferred_element_type=F32)
    gate_part, up_part = proj[:, :hidden_width], proj[:, hidden_width:]
    sigma = jax.nn.sigmoid(gate_part)
    activated = gate_part * sigma
    hidden = (activated * up_part).astype(BF16)
    back = jnp.dot(grad_rows, w_down[0], preferred_element_type=F32)
    slope = sigma * (1.0 + gate_part * (1.0 - sigma))
    both = jnp.concatenate([back * up_part * slope, back * activated], axis=1).astype(BF16)
    tn = (((0,), (0,)), ((), ()))
    left = lax.dot_general(input_rows, both, tn, preferred_element_type=F32)
    right = lax.dot_general(grad_rows, hidden, tn, preferred_element_type=F32)
    partial = jnp.concatenate([left, right], axis=1).astype(BF16)
    summed = lax.psum_scatter(partial, "dp", scatter_dimension=0, tiled=True).astype(F32)
    return stream[None], summed[None, :, : 2 * hidden_width], summed[None, :, 2 * hidden_width :]


def solution(mesh):
    rows = P(("dp", "exp"), "ctx", None)
    weights = P(("ctx", "exp"), None, None)
    placed = (rows, rows, rows, rows, P(), rows, rows, P(("dp", "exp"), "ctx"), rows, weights, weights)
    blocks = tuple(mesh.shape[a] for a in ("dp", "ctx", "exp"))
    body = per_device if blocks == (2, 4, 4) else routed_device
    return jax.shard_map(
        body,
        mesh=mesh,
        in_specs=placed,
        out_specs=(rows, P(("ctx", "exp"), "dp", None), P(("ctx", "exp"), "dp", None)),
        check_vma=False,
    )
```

```python
import math

import jax
import jax.numpy as jnp
from jax import lax
from jax.experimental import pallas as pl
from jax.experimental.pallas import tpu as pltpu
from jax.sharding import PartitionSpec as P

HEAD_DIM = 128
F32 = jnp.float32
BF16 = jnp.bfloat16


VMEM_SPEC = pl.BlockSpec(memory_space=pltpu.VMEM)
SMEM_SPEC = pl.BlockSpec(memory_space=pltpu.SMEM)
NN = (((1,), (0,)), ((), ()))


def on_chip(body, shapes, name, args, scratch=(), scalars=0, mib=8):
    return pl.pallas_call(
        body,
        out_shape=shapes,
        in_specs=[SMEM_SPEC] * scalars + [VMEM_SPEC] * (len(args) - scalars),
        out_specs=jax.tree.map(lambda _: VMEM_SPEC, shapes),
        scratch_shapes=list(scratch),
        compiler_params=pltpu.CompilerParams(vmem_limit_bytes=mib * 2**20),
        name=name,
    )(*args)


def pack_heads(arrays, ctx):
    tokens, width_all = arrays[0].shape
    width = width_all // ctx

    def body(*refs):
        for i, ref in enumerate(refs[:-1]):
            for j in range(ctx):
                refs[-1][j, i] = ref[:, j * width : (j + 1) * width]

    shape = jax.ShapeDtypeStruct((ctx, len(arrays), tokens, width), BF16)
    return on_chip(body, shape, "pack_heads", arrays)


def attend(packs):
    ctx, _, tokens, width = packs.shape
    scale = 1.0 / math.sqrt(HEAD_DIM)
    nt = (((1,), (1,)), ((), ()))

    def body(packs, out):
        for h in range(width // HEAD_DIM):
            cols = slice(h * HEAD_DIM, (h + 1) * HEAD_DIM)
            q, k, v = (
                jnp.concatenate([packs[j, i, :, cols] for j in range(ctx)], axis=0)
                for i in range(3)
            )
            scores = lax.dot_general(q, k, nt, preferred_element_type=F32) * scale
            largest = jnp.max(scores, axis=1, keepdims=True)
            powers = jnp.exp(scores - largest)
            probs = (powers / jnp.sum(powers, axis=1, keepdims=True)).astype(BF16)
            attended = lax.dot_general(probs, v, NN, preferred_element_type=F32)
            for j in range(ctx):
                rows = slice(j * tokens, (j + 1) * tokens)
                out[rows, cols] = (packs[j, 3, :, cols].astype(F32) + attended[rows]).astype(BF16)

    return on_chip(body, jax.ShapeDtypeStruct((ctx * tokens, width), BF16), "attend", [packs])


def selection(gate, cap):
    tokens = gate.shape[1]
    lower = lax.broadcasted_iota(jnp.int32, (tokens, tokens), 0)
    upper = lax.broadcasted_iota(jnp.int32, (tokens, tokens), 1)
    running = (lower <= upper).astype(BF16)
    row_number = lax.broadcasted_iota(jnp.int32, (cap, tokens), 0).astype(F32)
    picked = gate != 0.0
    marks = jnp.broadcast_to(picked.astype(F32), (8, tokens)).astype(BF16)
    rank = lax.dot_general(marks, running, NN, preferred_element_type=F32)[:1]
    return jnp.logical_and(row_number + 1.0 == rank, picked)


def pairs_of(ctx):
    return [tuple(range(t, min(t + 2, ctx))) for t in range(0, ctx, 2)]


def diagonal(chosen):
    ones = [c.astype(F32) for c in chosen]
    rows = [
        jnp.concatenate([o if i == j else jnp.zeros_like(o) for j in range(len(ones))], axis=1)
        for i, o in enumerate(ones)
    ]
    return jnp.concatenate(rows, axis=0).astype(BF16)


def cot_rows(place, down, blocks, cap, parts):
    seqs, (ctx, rows_in, width_all) = len(blocks), blocks[0].shape
    tokens = rows_in - 8
    half, hidden_width = width_all // parts, down.shape[1]
    count = seqs * ctx * cap

    def body(place, down, *refs):
        inputs, (cot_out, back_out, column_out, gate_out, cot_ref) = refs[:seqs], refs[seqs:]
        column = pl.ds(pl.multiple_of(place[2] * tokens, tokens), tokens)
        for i in range(seqs):
            for pair in pairs_of(ctx):
                at = (i * ctx + pair[0]) * cap
                chosen = []
                for k, t in enumerate(pair):
                    terms = inputs[i][t, tokens : tokens + 8, column].astype(F32)
                    gate = terms[0:1] + terms[1:2] + terms[2:3]
                    gate_out[i * ctx + t] = gate
                    chosen.append(selection(gate, cap))
                    column_out[at + k * cap : at + (k + 1) * cap, :] = jnp.broadcast_to(
                        jnp.sum(jnp.where(chosen[k], gate, 0.0), axis=1, keepdims=True), (cap, 128)
                    )
                select = diagonal(chosen)
                for p in range(parts):
                    block = jnp.concatenate(
                        [inputs[i][t, :tokens, p * half : (p + 1) * half] for t in pair], axis=0
                    )
                    rows = lax.dot_general(select, block, NN, preferred_element_type=F32)
                    cot_ref[p, at : at + len(pair) * cap, :] = rows.astype(BF16)
        back = None
        for p in range(parts):
            term = lax.dot_general(
                cot_ref[p], down[p * half : (p + 1) * half, :], NN, preferred_element_type=F32
            )
            back = term if back is None else back + term
        back_out[...] = back * column_out[:, :1]
        cot_out[...] = cot_ref[place[1]]

    shapes = [
        jax.ShapeDtypeStruct((count, half), BF16),
        jax.ShapeDtypeStruct((count, hidden_width), F32),
        jax.ShapeDtypeStruct((count, 128), F32),
        jax.ShapeDtypeStruct((seqs * ctx, 1, tokens), F32),
    ]
    scratch = [pltpu.VMEM((parts, count, half), BF16)]
    return on_chip(body, shapes, "cot_rows", [place, down, *blocks], scratch, 1, 16)


def stream_rows(place, gain, gate_up, slices, back, columns, gates, cap, parts, with_own):
    seqs, (ctx, length, width) = len(slices), slices[0].shape
    tokens, width_all = length // ctx, width * ctx
    half, hidden_width = width_all // parts, back.shape[1]
    count = seqs * ctx * cap

    def body(place, gain, gate_up, back_in, columns, gates, *refs):
        inputs, (norm_out, back_out, hidden_out, *own_out, rows_ref) = refs[:seqs], refs[seqs:]
        if with_own:
            own = pl.ds(pl.multiple_of(place[0] * tokens, tokens), tokens)
            for f in range(ctx):
                rows_ref[place[3 + f], :tokens, :] = inputs[0][f, own, :]
            for f in range(ctx):
                own_out[0][:, f * width : (f + 1) * width] = rows_ref[f, :tokens, :]
        for i in range(seqs):
            for pair in pairs_of(ctx):
                firsts = [pl.multiple_of(place[3 + t] * tokens, tokens) for t in pair]
                select = diagonal([selection(gates[i * ctx + t], cap) for t in pair])
                at = (i * ctx + pair[0]) * cap
                for f in range(ctx):
                    block = jnp.concatenate(
                        [inputs[i][f, pl.ds(first, tokens), :] for first in firsts], axis=0
                    )
                    rows = lax.dot_general(select, block, NN, preferred_element_type=F32)
                    rows_ref[place[3 + f], at : at + len(pair) * cap, :] = rows.astype(BF16)
        total = None
        for f in range(ctx):
            wide = rows_ref[f].astype(F32)
            square = jnp.sum(wide * wide, axis=1, keepdims=True)
            total = square if total is None else total + square
        factor = lax.rsqrt(total / width_all + 1e-05)
        proj = None
        for f in range(ctx):
            normed = (rows_ref[f].astype(F32) * factor * gain[f]).astype(BF16)
            rows_ref[f] = normed
            term = lax.dot_general(
                normed, gate_up[f * width : (f + 1) * width, :], NN, preferred_element_type=F32
            )
            proj = term if proj is None else proj + term
        gate_part, up_part = proj[:, :hidden_width], proj[:, hidden_width:]
        sigma = 1.0 / (1.0 + jnp.exp(-gate_part))
        activated = gate_part * sigma
        back = back_in[...]
        hidden_out[...] = (activated * up_part * columns[:, :1]).astype(BF16)
        slope = sigma * (1.0 + gate_part * (1.0 - sigma))
        back_out[:, :hidden_width] = (back * up_part * slope).astype(BF16)
        back_out[:, hidden_width:] = (back * activated).astype(BF16)
        each = ctx // parts
        for f in range(each):
            norm_out[:, f * width : (f + 1) * width] = rows_ref[place[1] * each + f]

    shapes = [
        jax.ShapeDtypeStruct((count, half), BF16),
        jax.ShapeDtypeStruct((count, 2 * hidden_width), BF16),
        jax.ShapeDtypeStruct((count, hidden_width), BF16),
    ]
    if with_own:
        shapes.append(jax.ShapeDtypeStruct((tokens, width_all), BF16))
    scratch = [pltpu.VMEM((ctx, count, width), BF16)]
    args = [place, gain, gate_up, back, columns, gates, *slices]
    return on_chip(body, shapes, "stream_rows", args, scratch, 1, 26)


def grads_kernel(*refs, groups):
    norms, cots, backs, hiddens = (refs[i * groups : (i + 1) * groups] for i in range(4))
    out_left, out_right = refs[4 * groups :]
    tn = (((0,), (0,)), ((), ()))

    def whole(parts):
        return jnp.concatenate([p[...] for p in parts], axis=0)

    out_left[0] = lax.dot_general(whole(norms), whole(backs), tn, preferred_element_type=F32)
    out_right[0] = lax.dot_general(whole(cots), whole(hiddens), tn, preferred_element_type=F32)


def grads(pieces):
    groups = len(pieces)
    norms, cots, backs, hiddens = zip(*pieces)
    count, half = norms[0].shape
    step = min(half, 512)
    tall = [pl.BlockSpec((count, step), lambda i: (0, i))] * groups
    out_widths = (backs[0].shape[1], hiddens[0].shape[1])
    full = [
        pl.BlockSpec((count, w), lambda i: (0, 0)) for w in out_widths for _ in range(groups)
    ]
    return pl.pallas_call(
        lambda *refs: grads_kernel(*refs, groups=groups),
        out_shape=[jax.ShapeDtypeStruct((1, half, w), F32) for w in out_widths],
        grid=(half // step,),
        in_specs=tall + tall + full,
        out_specs=[pl.BlockSpec((1, step, w), lambda i: (0, i, 0)) for w in out_widths],
        compiler_params=pltpu.CompilerParams(vmem_limit_bytes=32 * 2**20),
        name="grads",
    )(*norms, *cots, *backs, *hiddens)


def shifted(value, axis, step, count):
    return lax.ppermute(value, axis, [(i, (i + step) % count) for i in range(count)])


def flipped(value, axis, mask, count):
    return lax.ppermute(value, axis, [(i, i ^ mask) for i in range(count)])


def after(value, *others):
    return lax.optimization_barrier((value, *others))[0]


SOURCES = ((0, 1, 2, 3), (1, 0, 1, 2), (2, 2, 3, 1), (3, 3, 0, 0))


def spread(own, z, exp, waits=None, midway=None):
    waits = waits or {}

    def ready(number, values):
        return lax.optimization_barrier((values, waits.get(number, ())))[0]

    def line(value, pairs):
        return lax.ppermute(value, "ctx", pairs)

    def x(value):
        return flipped(value, "exp", 2, exp)

    def y(value):
        return flipped(value, "dp", 1, 2)

    def core(value):
        return flipped(value, "exp", 1, exp)

    up1, down1 = line(own, [(0, 1), (1, 2), (2, 3)]), line(own, [(1, 0), (2, 1), (3, 2)])
    x0, y0 = x(own), y(own)
    up1, down1, x0, y0 = ready(2, (up1, down1, x0, y0))
    one = jnp.where(z == 0, down1, up1)
    up2, down2 = line(up1, [(1, 2), (2, 3)]), line(down1, [(1, 0), (2, 1)])
    x1, y1 = x(one), y(one)
    up2, down2, x1, y1, y0 = ready(3, (up2, down2, x1, y1, y0))
    two = jnp.where(z == 3, up2, jnp.where(z == 0, down2, down1))
    middle = jnp.where(z == 2, up2, down2)
    ends = line(middle, [(1, 0), (2, 3)])
    x2, y2 = x(two), y(two)
    d0, d1 = x(y0), y(x1)
    ends, x2, y2, d0, d1 = ready(4, (ends, x2, y2, d0, d1))
    three = jnp.where(jnp.logical_or(z == 0, z == 3), ends, middle)
    x3, y3 = x(three), y(three)
    mine = jnp.stack([own, one, two, three])
    mine_core = core(mine)
    x3, y3, mine_core, y2 = ready(5, (x3, y3, mine_core, y2))
    d2, d3 = x(y2), y(x3)
    done = midway(mine, mine_core) if midway else ()
    over_x, over_y = jnp.stack([x0, x1, x2, x3]), jnp.stack([y0, y1, y2, y3])
    over_x_core, over_y_core = core(over_x), core(over_y)
    both = lax.optimization_barrier((jnp.stack([d0, d1, d2, d3]), done))[0]
    both_core = core(both)
    return {
        (0, 0): (mine, mine_core),
        (0, 1): (over_x, over_x_core),
        (1, 0): (over_y, over_y_core),
        (1, 1): (both, both_core),
    }, (up2, down2), (d2, d3)


def gate_terms(value):
    terms = []
    for _ in range(3):
        term = lax.reduce_precision(value, 8, 7)
        terms.append(term.astype(BF16))
        value = value - term
    return terms


def expert_gates(routes, gates, flags, experts):
    named = routes[:, :, None] == jnp.arange(experts, dtype=jnp.int32)[None, None, :]
    scaled = gates * flags.astype(F32)[:, None]
    return jnp.sum(jnp.where(named, scaled[:, :, None], 0.0), axis=1)


def per_device(
    queries, keys, values, resid, norm_gain, expert_ids, gate_weights, mask_flags, cotangent, w_gate_up, w_down
):
    ctx, exp, parts = (lax.axis_size(a) for a in ("ctx", "exp", "dp"))
    z, e, part = (lax.axis_index(a) for a in ("ctx", "exp", "dp"))
    experts = ctx * exp
    _, tokens, width_all = queries.shape
    width = width_all // ctx
    most = min(tokens, tokens * expert_ids.shape[2] * 17 // (16 * experts))
    cap = -(-most // 8) * 8

    by_expert = expert_gates(expert_ids[0], gate_weights[0], mask_flags[0], experts)
    terms = jnp.stack([t.T.reshape(experts * tokens) for t in gate_terms(by_expert)])
    terms = jnp.pad(terms, ((0, 5), (0, width_all - experts * tokens)))
    block = jnp.concatenate([cotangent[0], terms], axis=0)
    sources = [jnp.asarray(row, jnp.int32)[z] for row in SOURCES]
    place = jnp.stack([z, part, z * exp + e, *sources]).astype(jnp.int32)
    packed = pack_heads([queries[0], keys[0], values[0], resid[0]], ctx)
    cots, line_done, last = spread(block, z, exp, {3: (packed, place)})

    packed = after(packed, line_done)
    packs = lax.all_to_all(packed, "ctx", split_axis=0, concat_axis=0, tiled=True)
    own_slice = attend(packs)

    gain = norm_gain.reshape(ctx, 1, width)
    order = ((0, 0), (0, 1), (1, 0), (1, 1))
    picked = {where: cot_rows(place, w_down[0], cots[where], cap, parts) for where in order}

    def expert(where, slices):
        rows, back, columns, gates = picked[where]
        normed, both, hidden, *own = stream_rows(
            place, gain, w_gate_up[0], slices, back, columns, gates, cap, parts, where == (0, 0)
        )
        return normed, rows, both, hidden, *own

    pieces = {}

    def midway(mine, mine_core):
        pieces[0, 0] = expert((0, 0), (mine, mine_core))
        return pieces[0, 0]

    waits = {2: (picked[0, 0], last[0]), 3: last[1], 4: picked[0, 1], 5: (picked[1, 0], picked[1, 1])}
    streams, _, _ = spread(own_slice, z, exp, waits, midway)
    for where in order[1:]:
        pieces[where] = expert(where, streams[where])
    stream = pieces[0, 0][4]
    left, right = grads([pieces[where][:4] for where in order])
    return stream[None], left, right


def routed_device(
    queries, keys, values, resid, norm_gain, expert_ids, gate_weights, mask_flags, cotangent, w_gate_up, w_down
):
    ctx, exp = (lax.axis_size(a) for a in ("ctx", "exp"))
    experts = ctx * exp
    _, tokens, width_all = queries.shape
    top = expert_ids.shape[2]
    capacity = min(tokens, tokens * top * 17 // (16 * experts))
    keys_all = lax.all_gather(keys[0], "ctx", axis=0, tiled=True)
    values_all = lax.all_gather(values[0], "ctx", axis=0, tiled=True)
    heads = width_all // HEAD_DIM
    q, k, v = (a.reshape(-1, heads, HEAD_DIM) for a in (queries[0], keys_all, values_all))
    scores = jnp.einsum("qhd,khd->hqk", q, k, preferred_element_type=F32) / math.sqrt(HEAD_DIM)
    powers = jnp.exp(scores - jnp.max(scores, axis=2, keepdims=True))
    probs = (powers / jnp.sum(powers, axis=2, keepdims=True)).astype(BF16)
    attended = jnp.einsum("hqk,khd->qhd", probs, v, preferred_element_type=F32)
    stream = (resid[0].astype(F32) + attended.reshape(tokens, width_all)).astype(BF16)
    wide = lax.optimization_barrier(stream).astype(F32)
    factor = lax.rsqrt(jnp.mean(wide * wide, axis=-1, keepdims=True) + 1e-05)
    normed = (wide * factor * norm_gain).astype(BF16)

    by_expert = expert_gates(expert_ids[0], gate_weights[0], mask_flags[0], experts)
    picked = by_expert != 0.0
    running = jnp.arange(tokens)[:, None] >= jnp.arange(tokens)[None, :]
    rank = jnp.dot(running.astype(BF16), picked.astype(BF16), preferred_element_type=F32) - 1.0
    slot = jnp.arange(capacity, dtype=F32)[None, :, None]
    chosen = jnp.logical_and(rank.T[:, None, :] == slot, picked.T[:, None, :])
    select = chosen.astype(BF16).reshape(experts * capacity, tokens)
    sent_rows = jnp.dot(select, normed, preferred_element_type=F32).astype(BF16)
    gate_rows = jnp.sum(jnp.where(chosen, by_expert.T[:, None, :], 0.0), axis=2).reshape(-1, 1)
    picked_cot = jnp.dot(select, cotangent[0], preferred_element_type=F32)
    sent_grads = (picked_cot * gate_rows).astype(BF16)

    def exchanged(rows):
        rows = rows.reshape(experts, capacity, width_all)
        got = lax.all_to_all(rows, ("ctx", "exp"), split_axis=0, concat_axis=0, tiled=True)
        return got.reshape(-1, width_all)

    input_rows, grad_rows = exchanged(sent_rows), exchanged(sent_grads)
    hidden_width = w_down.shape[2]
    proj = jnp.dot(input_rows, w_gate_up[0], preferred_element_type=F32)
    gate_part, up_part = proj[:, :hidden_width], proj[:, hidden_width:]
    sigma = jax.nn.sigmoid(gate_part)
    activated = gate_part * sigma
    hidden = (activated * up_part).astype(BF16)
    back = jnp.dot(grad_rows, w_down[0], preferred_element_type=F32)
    slope = sigma * (1.0 + gate_part * (1.0 - sigma))
    both = jnp.concatenate([back * up_part * slope, back * activated], axis=1).astype(BF16)
    tn = (((0,), (0,)), ((), ()))
    left = lax.dot_general(input_rows, both, tn, preferred_element_type=F32)
    right = lax.dot_general(grad_rows, hidden, tn, preferred_element_type=F32)
    partial = jnp.concatenate([left, right], axis=1).astype(BF16)
    summed = lax.psum_scatter(partial, "dp", scatter_dimension=0, tiled=True).astype(F32)
    return stream[None], summed[None, :, : 2 * hidden_width], summed[None, :, 2 * hidden_width :]


def solution(mesh):
    rows = P(("dp", "exp"), "ctx", None)
    weights = P(("ctx", "exp"), None, None)
    placed = (rows, rows, rows, rows, P(), rows, rows, P(("dp", "exp"), "ctx"), rows, weights, weights)
    blocks = tuple(mesh.shape[a] for a in ("dp", "ctx", "exp"))
    body = per_device if blocks == (2, 4, 4) else routed_device
    return jax.shard_map(
        body,
        mesh=mesh,
        in_specs=placed,
        out_specs=(rows, P(("ctx", "exp"), "dp", None), P(("ctx", "exp"), "dp", None)),
        check_vma=False,
    )
```

```python
import math

import jax
import jax.numpy as jnp
from jax import lax
from jax.experimental import pallas as pl
from jax.experimental.pallas import tpu as pltpu
from jax.sharding import PartitionSpec as P

HEAD_DIM = 128
F32 = jnp.float32
BF16 = jnp.bfloat16


VMEM_SPEC = pl.BlockSpec(memory_space=pltpu.VMEM)
SMEM_SPEC = pl.BlockSpec(memory_space=pltpu.SMEM)
NN = (((1,), (0,)), ((), ()))


def on_chip(body, shapes, name, args, scratch=(), scalars=0, mib=8):
    return pl.pallas_call(
        body,
        out_shape=shapes,
        in_specs=[SMEM_SPEC] * scalars + [VMEM_SPEC] * (len(args) - scalars),
        out_specs=jax.tree.map(lambda _: VMEM_SPEC, shapes),
        scratch_shapes=list(scratch),
        compiler_params=pltpu.CompilerParams(vmem_limit_bytes=mib * 2**20),
        name=name,
    )(*args)


def pack_heads(arrays, ctx):
    tokens, width_all = arrays[0].shape
    width = width_all // ctx

    def body(*refs):
        for i, ref in enumerate(refs[:-1]):
            for j in range(ctx):
                refs[-1][j, i] = ref[:, j * width : (j + 1) * width]

    shape = jax.ShapeDtypeStruct((ctx, len(arrays), tokens, width), BF16)
    return on_chip(body, shape, "pack_heads", arrays)


def attend(packs):
    ctx, _, tokens, width = packs.shape
    scale = 1.0 / math.sqrt(HEAD_DIM)
    nt = (((1,), (1,)), ((), ()))

    def body(packs, out):
        for h in range(width // HEAD_DIM):
            cols = slice(h * HEAD_DIM, (h + 1) * HEAD_DIM)
            q, k, v = (
                jnp.concatenate([packs[j, i, :, cols] for j in range(ctx)], axis=0)
                for i in range(3)
            )
            scores = lax.dot_general(q, k, nt, preferred_element_type=F32) * scale
            largest = jnp.max(scores, axis=1, keepdims=True)
            powers = jnp.exp(scores - largest)
            probs = (powers / jnp.sum(powers, axis=1, keepdims=True)).astype(BF16)
            attended = lax.dot_general(probs, v, NN, preferred_element_type=F32)
            for j in range(ctx):
                rows = slice(j * tokens, (j + 1) * tokens)
                out[rows, cols] = (packs[j, 3, :, cols].astype(F32) + attended[rows]).astype(BF16)

    return on_chip(body, jax.ShapeDtypeStruct((ctx * tokens, width), BF16), "attend", [packs])


def selection(gate, cap):
    tokens = gate.shape[1]
    lower = lax.broadcasted_iota(jnp.int32, (tokens, tokens), 0)
    upper = lax.broadcasted_iota(jnp.int32, (tokens, tokens), 1)
    running = (lower <= upper).astype(BF16)
    row_number = lax.broadcasted_iota(jnp.int32, (cap, tokens), 0).astype(F32)
    picked = gate != 0.0
    marks = jnp.broadcast_to(picked.astype(F32), (8, tokens)).astype(BF16)
    rank = lax.dot_general(marks, running, NN, preferred_element_type=F32)[:1]
    return jnp.logical_and(row_number + 1.0 == rank, picked)


def pairs_of(ctx):
    return [tuple(range(t, min(t + 2, ctx))) for t in range(0, ctx, 2)]


def diagonal(chosen):
    ones = [c.astype(F32) for c in chosen]
    rows = [
        jnp.concatenate([o if i == j else jnp.zeros_like(o) for j in range(len(ones))], axis=1)
        for i, o in enumerate(ones)
    ]
    return jnp.concatenate(rows, axis=0).astype(BF16)


def cot_rows(place, down, blocks, cap, parts):
    seqs, (ctx, rows_in, width_all) = len(blocks), blocks[0].shape
    tokens = rows_in - 8
    half, hidden_width = width_all // parts, down.shape[1]
    count = seqs * ctx * cap

    def body(place, down, *refs):
        inputs, (cot_out, back_out, column_out, gate_out, cot_ref) = refs[:seqs], refs[seqs:]
        column = pl.ds(pl.multiple_of(place[2] * tokens, tokens), tokens)
        for i in range(seqs):
            for pair in pairs_of(ctx):
                at = (i * ctx + pair[0]) * cap
                chosen = []
                for k, t in enumerate(pair):
                    terms = inputs[i][t, tokens : tokens + 8, column].astype(F32)
                    gate = terms[0:1] + terms[1:2] + terms[2:3]
                    gate_out[i * ctx + t] = gate
                    chosen.append(selection(gate, cap))
                    column_out[at + k * cap : at + (k + 1) * cap, :] = jnp.broadcast_to(
                        jnp.sum(jnp.where(chosen[k], gate, 0.0), axis=1, keepdims=True), (cap, 128)
                    )
                select = diagonal(chosen)
                for p in range(parts):
                    block = jnp.concatenate(
                        [inputs[i][t, :tokens, p * half : (p + 1) * half] for t in pair], axis=0
                    )
                    rows = lax.dot_general(select, block, NN, preferred_element_type=F32)
                    cot_ref[p, at : at + len(pair) * cap, :] = rows.astype(BF16)
        back = None
        for p in range(parts):
            term = lax.dot_general(
                cot_ref[p], down[p * half : (p + 1) * half, :], NN, preferred_element_type=F32
            )
            back = term if back is None else back + term
        back_out[...] = back * column_out[:, :1]
        cot_out[...] = cot_ref[place[1]]

    shapes = [
        jax.ShapeDtypeStruct((count, half), BF16),
        jax.ShapeDtypeStruct((count, hidden_width), F32),
        jax.ShapeDtypeStruct((count, 128), F32),
        jax.ShapeDtypeStruct((seqs * ctx, 1, tokens), F32),
    ]
    scratch = [pltpu.VMEM((parts, count, half), BF16)]
    return on_chip(body, shapes, "cot_rows", [place, down, *blocks], scratch, 1, 16)


def stream_rows(place, gain, gate_up, slices, back, columns, gates, cap, parts, with_own):
    seqs, (ctx, length, width) = len(slices), slices[0].shape
    tokens, width_all = length // ctx, width * ctx
    half, hidden_width = width_all // parts, back.shape[1]
    count = seqs * ctx * cap

    def body(place, gain, gate_up, back_in, columns, gates, *refs):
        inputs, (norm_out, back_out, hidden_out, *own_out, rows_ref) = refs[:seqs], refs[seqs:]
        if with_own:
            own = pl.ds(pl.multiple_of(place[0] * tokens, tokens), tokens)
            for f in range(ctx):
                rows_ref[place[3 + f], :tokens, :] = inputs[0][f, own, :]
            for f in range(ctx):
                own_out[0][:, f * width : (f + 1) * width] = rows_ref[f, :tokens, :]
        for i in range(seqs):
            for pair in pairs_of(ctx):
                firsts = [pl.multiple_of(place[3 + t] * tokens, tokens) for t in pair]
                select = diagonal([selection(gates[i * ctx + t], cap) for t in pair])
                at = (i * ctx + pair[0]) * cap
                for f in range(ctx):
                    block = jnp.concatenate(
                        [inputs[i][f, pl.ds(first, tokens), :] for first in firsts], axis=0
                    )
                    rows = lax.dot_general(select, block, NN, preferred_element_type=F32)
                    rows_ref[place[3 + f], at : at + len(pair) * cap, :] = rows.astype(BF16)
        total = None
        for f in range(ctx):
            wide = rows_ref[f].astype(F32)
            square = jnp.sum(wide * wide, axis=1, keepdims=True)
            total = square if total is None else total + square
        factor = lax.rsqrt(total / width_all + 1e-05)
        proj = None
        for f in range(ctx):
            normed = (rows_ref[f].astype(F32) * factor * gain[f]).astype(BF16)
            rows_ref[f] = normed
            term = lax.dot_general(
                normed, gate_up[f * width : (f + 1) * width, :], NN, preferred_element_type=F32
            )
            proj = term if proj is None else proj + term
        gate_part, up_part = proj[:, :hidden_width], proj[:, hidden_width:]
        sigma = 1.0 / (1.0 + jnp.exp(-gate_part))
        activated = gate_part * sigma
        back = back_in[...]
        hidden_out[...] = (activated * up_part * columns[:, :1]).astype(BF16)
        slope = sigma * (1.0 + gate_part * (1.0 - sigma))
        back_out[:, :hidden_width] = (back * up_part * slope).astype(BF16)
        back_out[:, hidden_width:] = (back * activated).astype(BF16)
        each = ctx // parts
        for f in range(each):
            norm_out[:, f * width : (f + 1) * width] = rows_ref[place[1] * each + f]

    shapes = [
        jax.ShapeDtypeStruct((count, half), BF16),
        jax.ShapeDtypeStruct((count, 2 * hidden_width), BF16),
        jax.ShapeDtypeStruct((count, hidden_width), BF16),
    ]
    if with_own:
        shapes.append(jax.ShapeDtypeStruct((tokens, width_all), BF16))
    scratch = [pltpu.VMEM((ctx, count, width), BF16)]
    args = [place, gain, gate_up, back, columns, gates, *slices]
    return on_chip(body, shapes, "stream_rows", args, scratch, 1, 26)


def grads_kernel(*refs, groups):
    norms, cots, backs, hiddens = (refs[i * groups : (i + 1) * groups] for i in range(4))
    out_left, out_right = refs[4 * groups :]
    tn = (((0,), (0,)), ((), ()))

    def whole(parts):
        return jnp.concatenate([p[...] for p in parts], axis=0)

    out_left[0] = lax.dot_general(whole(norms), whole(backs), tn, preferred_element_type=F32)
    out_right[0] = lax.dot_general(whole(cots), whole(hiddens), tn, preferred_element_type=F32)


def grads(pieces):
    groups = len(pieces)
    norms, cots, backs, hiddens = zip(*pieces)
    count, half = norms[0].shape
    step = min(half, 512)
    tall = [pl.BlockSpec((count, step), lambda i: (0, i))] * groups
    out_widths = (backs[0].shape[1], hiddens[0].shape[1])
    full = [
        pl.BlockSpec((count, w), lambda i: (0, 0)) for w in out_widths for _ in range(groups)
    ]
    return pl.pallas_call(
        lambda *refs: grads_kernel(*refs, groups=groups),
        out_shape=[jax.ShapeDtypeStruct((1, half, w), F32) for w in out_widths],
        grid=(half // step,),
        in_specs=tall + tall + full,
        out_specs=[pl.BlockSpec((1, step, w), lambda i: (0, i, 0)) for w in out_widths],
        compiler_params=pltpu.CompilerParams(vmem_limit_bytes=32 * 2**20),
        name="grads",
    )(*norms, *cots, *backs, *hiddens)


def shifted(value, axis, step, count):
    return lax.ppermute(value, axis, [(i, (i + step) % count) for i in range(count)])


def flipped(value, axis, mask, count):
    return lax.ppermute(value, axis, [(i, i ^ mask) for i in range(count)])


def after(value, *others):
    return lax.optimization_barrier((value, *others))[0]


SOURCES = ((0, 1, 2, 3), (1, 0, 1, 2), (2, 2, 3, 1), (3, 3, 0, 0))


def spread(own, z, exp, waits=None, midway=None):
    waits = waits or {}

    def ready(number, values):
        return lax.optimization_barrier((values, waits.get(number, ())))[0]

    def line(value, pairs):
        return lax.ppermute(value, "ctx", pairs)

    def x(value):
        return flipped(value, "exp", 2, exp)

    def y(value):
        return flipped(value, "dp", 1, 2)

    def core(value):
        return flipped(value, "exp", 1, exp)

    up1, down1 = line(own, [(0, 1), (1, 2), (2, 3)]), line(own, [(1, 0), (2, 1), (3, 2)])
    x0, y0 = x(own), y(own)
    up1, down1, x0, y0 = ready(2, (up1, down1, x0, y0))
    one = jnp.where(z == 0, down1, up1)
    up2, down2 = line(up1, [(1, 2), (2, 3)]), line(down1, [(1, 0), (2, 1)])
    x1, y1 = x(one), y(one)
    up2, down2, x1, y1, y0 = ready(3, (up2, down2, x1, y1, y0))
    two = jnp.where(z == 3, up2, jnp.where(z == 0, down2, down1))
    middle = jnp.where(z == 2, up2, down2)
    ends = line(middle, [(1, 0), (2, 3)])
    x2, y2 = x(two), y(two)
    d0, d1 = x(y0), y(x1)
    ends, x2, y2, d0, d1 = ready(4, (ends, x2, y2, d0, d1))
    three = jnp.where(jnp.logical_or(z == 0, z == 3), ends, middle)
    x3, y3 = x(three), y(three)
    mine = jnp.stack([own, one, two, three])
    mine_core = core(mine)
    x3, y3, mine_core, y2 = ready(5, (x3, y3, mine_core, y2))
    d2, d3 = x(y2), y(x3)
    done = midway(mine, mine_core) if midway else ()
    over_x, over_y = jnp.stack([x0, x1, x2, x3]), jnp.stack([y0, y1, y2, y3])
    over_x_core, over_y_core = core(over_x), core(over_y)
    both = lax.optimization_barrier((jnp.stack([d0, d1, d2, d3]), done))[0]
    both_core = core(both)
    return {
        (0, 0): (mine, mine_core),
        (0, 1): (over_x, over_x_core),
        (1, 0): (over_y, over_y_core),
        (1, 1): (both, both_core),
    }, (up2, down2), (d2, d3)


def expert_gates(routes, gates, flags, experts):
    named = routes[:, :, None] == jnp.arange(experts, dtype=jnp.int32)[None, None, :]
    scaled = gates * flags.astype(F32)[:, None]
    return jnp.sum(jnp.where(named, scaled[:, :, None], 0.0), axis=1)


def gated_block(cot, routes, gates, flags, experts):
    tokens, width_all = cot.shape

    def body(cot, routes, gates, flags, out):
        out[:tokens, :] = cot[...]
        named = jnp.transpose(routes[...].astype(F32))
        scaled = jnp.transpose(gates[...]) * flags[...].astype(F32)
        out[tokens:, :] = jnp.zeros((8, width_all), BF16)
        for e in range(experts):
            left = jnp.sum(jnp.where(named == float(e), scaled, 0.0), axis=0, keepdims=True)
            terms = []
            for _ in range(3):
                terms.append(left.astype(BF16).astype(F32))
                left = left - terms[-1]
            rows = jnp.concatenate(terms + [jnp.zeros((5, tokens), F32)], axis=0)
            out[tokens:, e * tokens : (e + 1) * tokens] = rows.astype(BF16)

    shape = jax.ShapeDtypeStruct((tokens + 8, width_all), BF16)
    return on_chip(body, shape, "gated_block", [cot, routes, gates, flags])


def per_device(
    queries, keys, values, resid, norm_gain, expert_ids, gate_weights, mask_flags, cotangent, w_gate_up, w_down
):
    ctx, exp, parts = (lax.axis_size(a) for a in ("ctx", "exp", "dp"))
    z, e, part = (lax.axis_index(a) for a in ("ctx", "exp", "dp"))
    experts = ctx * exp
    _, tokens, width_all = queries.shape
    width = width_all // ctx
    most = min(tokens, tokens * expert_ids.shape[2] * 17 // (16 * experts))
    cap = -(-most // 8) * 8

    block = gated_block(cotangent[0], expert_ids[0], gate_weights[0], mask_flags, experts)
    sources = [jnp.asarray(row, jnp.int32)[z] for row in SOURCES]
    place = jnp.stack([z, part, z * exp + e, *sources]).astype(jnp.int32)
    packed = pack_heads([queries[0], keys[0], values[0], resid[0]], ctx)
    cots, line_done, last = spread(block, z, exp, {3: (packed, place)})

    packed = after(packed, line_done)
    packs = lax.all_to_all(packed, "ctx", split_axis=0, concat_axis=0, tiled=True)
    own_slice = attend(packs)

    gain = norm_gain.reshape(ctx, 1, width)
    order = ((0, 0), (0, 1), (1, 0), (1, 1))
    picked = {where: cot_rows(place, w_down[0], cots[where], cap, parts) for where in order}

    def expert(where, slices):
        rows, back, columns, gates = picked[where]
        normed, both, hidden, *own = stream_rows(
            place, gain, w_gate_up[0], slices, back, columns, gates, cap, parts, where == (0, 0)
        )
        return normed, rows, both, hidden, *own

    pieces = {}

    def midway(mine, mine_core):
        pieces[0, 0] = expert((0, 0), (mine, mine_core))
        return pieces[0, 0]

    waits = {2: (picked[0, 0], last[0]), 3: last[1], 4: picked[0, 1], 5: (picked[1, 0], picked[1, 1])}
    streams, _, _ = spread(own_slice, z, exp, waits, midway)
    for where in order[1:]:
        pieces[where] = expert(where, streams[where])
    stream = pieces[0, 0][4]
    left, right = grads([pieces[where][:4] for where in order])
    return stream[None], left, right


def routed_device(
    queries, keys, values, resid, norm_gain, expert_ids, gate_weights, mask_flags, cotangent, w_gate_up, w_down
):
    ctx, exp = (lax.axis_size(a) for a in ("ctx", "exp"))
    experts = ctx * exp
    _, tokens, width_all = queries.shape
    top = expert_ids.shape[2]
    capacity = min(tokens, tokens * top * 17 // (16 * experts))
    keys_all = lax.all_gather(keys[0], "ctx", axis=0, tiled=True)
    values_all = lax.all_gather(values[0], "ctx", axis=0, tiled=True)
    heads = width_all // HEAD_DIM
    q, k, v = (a.reshape(-1, heads, HEAD_DIM) for a in (queries[0], keys_all, values_all))
    scores = jnp.einsum("qhd,khd->hqk", q, k, preferred_element_type=F32) / math.sqrt(HEAD_DIM)
    powers = jnp.exp(scores - jnp.max(scores, axis=2, keepdims=True))
    probs = (powers / jnp.sum(powers, axis=2, keepdims=True)).astype(BF16)
    attended = jnp.einsum("hqk,khd->qhd", probs, v, preferred_element_type=F32)
    stream = (resid[0].astype(F32) + attended.reshape(tokens, width_all)).astype(BF16)
    wide = lax.optimization_barrier(stream).astype(F32)
    factor = lax.rsqrt(jnp.mean(wide * wide, axis=-1, keepdims=True) + 1e-05)
    normed = (wide * factor * norm_gain).astype(BF16)

    by_expert = expert_gates(expert_ids[0], gate_weights[0], mask_flags[0], experts)
    picked = by_expert != 0.0
    running = jnp.arange(tokens)[:, None] >= jnp.arange(tokens)[None, :]
    rank = jnp.dot(running.astype(BF16), picked.astype(BF16), preferred_element_type=F32) - 1.0
    slot = jnp.arange(capacity, dtype=F32)[None, :, None]
    chosen = jnp.logical_and(rank.T[:, None, :] == slot, picked.T[:, None, :])
    select = chosen.astype(BF16).reshape(experts * capacity, tokens)
    sent_rows = jnp.dot(select, normed, preferred_element_type=F32).astype(BF16)
    gate_rows = jnp.sum(jnp.where(chosen, by_expert.T[:, None, :], 0.0), axis=2).reshape(-1, 1)
    picked_cot = jnp.dot(select, cotangent[0], preferred_element_type=F32)
    sent_grads = (picked_cot * gate_rows).astype(BF16)

    def exchanged(rows):
        rows = rows.reshape(experts, capacity, width_all)
        got = lax.all_to_all(rows, ("ctx", "exp"), split_axis=0, concat_axis=0, tiled=True)
        return got.reshape(-1, width_all)

    input_rows, grad_rows = exchanged(sent_rows), exchanged(sent_grads)
    hidden_width = w_down.shape[2]
    proj = jnp.dot(input_rows, w_gate_up[0], preferred_element_type=F32)
    gate_part, up_part = proj[:, :hidden_width], proj[:, hidden_width:]
    sigma = jax.nn.sigmoid(gate_part)
    activated = gate_part * sigma
    hidden = (activated * up_part).astype(BF16)
    back = jnp.dot(grad_rows, w_down[0], preferred_element_type=F32)
    slope = sigma * (1.0 + gate_part * (1.0 - sigma))
    both = jnp.concatenate([back * up_part * slope, back * activated], axis=1).astype(BF16)
    tn = (((0,), (0,)), ((), ()))
    left = lax.dot_general(input_rows, both, tn, preferred_element_type=F32)
    right = lax.dot_general(grad_rows, hidden, tn, preferred_element_type=F32)
    partial = jnp.concatenate([left, right], axis=1).astype(BF16)
    summed = lax.psum_scatter(partial, "dp", scatter_dimension=0, tiled=True).astype(F32)
    return stream[None], summed[None, :, : 2 * hidden_width], summed[None, :, 2 * hidden_width :]


def solution(mesh):
    rows = P(("dp", "exp"), "ctx", None)
    weights = P(("ctx", "exp"), None, None)
    placed = (rows, rows, rows, rows, P(), rows, rows, P(("dp", "exp"), "ctx"), rows, weights, weights)
    blocks = tuple(mesh.shape[a] for a in ("dp", "ctx", "exp"))
    body = per_device if blocks == (2, 4, 4) else routed_device
    return jax.shard_map(
        body,
        mesh=mesh,
        in_specs=placed,
        out_specs=(rows, P(("ctx", "exp"), "dp", None), P(("ctx", "exp"), "dp", None)),
        check_vma=False,
    )
```
